128 devices in a mesh: blk: 32 (over z, y, core), pen: 4 (over x).
Axes of the slice: x: 4, y: 4, z: 4, core: 2. Of those that a mesh axis runs over, the one named last changes fastest.
Arguments:
- snapshots: bfloat16 [4, 512, 2048, 128], P(None, ('blk', 'pen')), may hold values from -110 to 110
- start_time: float32 [128, 64], replicated, may hold values from -6 to 6
- start_plane: float32 [512, 32], replicated, may hold values from -6 to 6
Outputs:
- time_basis: float32 [128, 64], replicated
- plane_basis: float32 [512, 32], replicated
- core_tensor: bfloat16 [4, 32, 131072], P(None, None, ('blk', 'pen'))
The draws below stay inside these ranges and needn't reach their ends.
All inputs are finite; a program needn't handle non-finite values.
Results may differ from the reference program's by a relative error of at most 0.005.
Values may be sent and summed in bfloat16 or wider, within the bound.
No kernel may reach another device: no remote copies, remote signals or barrier semaphores. Data moves between devices by JAX's collectives and lax.ppermute only.
A program may use at most 64 MiB of HBM per device.

```python
import math
import jax
import jax.numpy as jnp
from jax import lax

VARS = 4
NX = 512
TSTEPS = 128
RANK_T = 64
RANK_X = 32
ITT = 3
ITX = 3
YZ = 2048


def draw_snapshots(key, part):
    key_list = jax.random.split(key, 6)
    plane_index = jnp.arange(NX, dtype=jnp.float32).reshape(1, NX, 1, 1)
    cell_index = jnp.arange(YZ, dtype=jnp.float32).reshape(1, 1, YZ, 1)
    step_index = jnp.arange(TSTEPS, dtype=jnp.float32).reshape(1, 1, 1, TSTEPS)
    ramp_scale = jnp.exp(jnp.log(3.0) * (plane_index / max(NX - 1, 1) + cell_index / max(YZ - 1, 1)))
    rough_scale = jnp.exp(jax.random.uniform(key_list[0], (VARS, NX, YZ, 1), jnp.float32, 0.0, math.log(10.0)))
    noise_part = jnp.clip(jax.random.normal(key_list[1], (VARS, NX, YZ, TSTEPS), jnp.float32), -6.0, 6.0)
    step_scale = jnp.exp(jax.random.uniform(key_list[2], (VARS, 1, 1, TSTEPS), jnp.float32, 0.0, math.log(3.0)))
    wave_number = jax.random.randint(key_list[3], (VARS, 1, YZ, 1), 1, 9).astype(jnp.float32)
    angular_rate = jax.random.uniform(key_list[4], (VARS, 1, YZ, 1), jnp.float32, 0.05, 0.6)
    wave_phase = jax.random.uniform(key_list[5], (VARS, 1, YZ, 1), jnp.float32, -math.pi, math.pi)
    wave_part = jnp.cos(2.0 * math.pi * wave_number * plane_index / NX + angular_rate * step_index + wave_phase)
    result = rough_scale * ramp_scale * step_scale * (noise_part + 1.5 * wave_part) / 20.0
    return result.astype(jnp.bfloat16)


def gaussian(key, shape, width, bound, kind=jnp.bfloat16):
    return jnp.clip(width * jax.random.normal(key, shape, jnp.float32), -bound, bound).astype(kind)


def setup_inputs(seed: int = 0) -> dict:
    splits = jax.random.split(jax.random.key(seed), 4)
    return {
        "snapshots": draw_snapshots(jax.random.fold_in(splits[3], 71), 0),
        "start_time": gaussian(splits[1], (TSTEPS, RANK_T), 1.0, 6.0, jnp.float32),
        "start_plane": gaussian(splits[2], (NX, RANK_X), 1.0, 6.0, jnp.float32),
    }


HIGHEST = lax.Precision.HIGHEST

def orthonormal(matrix):
    for repeat in range(2):
        square_gram = jnp.dot(matrix.T, matrix, precision=HIGHEST)
        lower_factor = jnp.linalg.cholesky(square_gram)
        matrix = jax.scipy.linalg.solve_triangular(lower_factor, matrix.T, lower=True).T
    return matrix

def subspace(operator_gram, initial, sweeps):
    current = initial
    for repeat in range(sweeps):
        current = orthonormal(jnp.dot(operator_gram, current, precision=HIGHEST))
    return current

def reference(snapshots, start_time, start_plane):
    gram_time = jnp.zeros((TSTEPS, TSTEPS), jnp.float32)
    for variable in range(VARS):
        row_matrix = snapshots[variable].reshape(NX * YZ, TSTEPS)
        gram_time = gram_time + jnp.dot(row_matrix.T.astype(jnp.float32), row_matrix.astype(jnp.float32), preferred_element_type=jnp.float32)
    gram_time = gram_time / (VARS * NX * YZ)
    time_basis = subspace(gram_time, start_time, ITT)
    time_narrow = time_basis.astype(jnp.bfloat16)
    core_parts = []
    gram_plane = jnp.zeros((NX, NX), jnp.float32)
    for variable in range(VARS):
        row_matrix = snapshots[variable].reshape(NX * YZ, TSTEPS)
        core_part = jnp.dot(row_matrix.astype(jnp.float32), time_narrow.astype(jnp.float32), preferred_element_type=jnp.float32).astype(jnp.bfloat16)
        core_part = core_part.reshape(NX, YZ * RANK_T)
        gram_plane = gram_plane + jnp.dot(core_part.astype(jnp.float32), core_part.T.astype(jnp.float32), preferred_element_type=jnp.float32)
        core_parts.append(core_part)
    gram_plane = gram_plane / (VARS * YZ * RANK_T)
    plane_basis = subspace(gram_plane, start_plane, ITX)
    plane_narrow = plane_basis.astype(jnp.bfloat16)
    core_tensor = jnp.stack([jnp.dot(plane_narrow.T.astype(jnp.float32), core_part.astype(jnp.float32), preferred_element_type=jnp.float32).astype(jnp.bfloat16) for core_part in core_parts])
    return (time_basis, plane_basis, core_tensor)
```

```python
import jax
import jax.numpy as jnp
from jax import lax
from jax.sharding import PartitionSpec as P

ITT = 3
ITX = 3


HIGHEST = lax.Precision.HIGHEST


def orthonormal(matrix):
    for repeat in range(2):
        square_gram = jnp.dot(matrix.T, matrix, precision=HIGHEST)
        lower_factor = jnp.linalg.cholesky(square_gram)
        matrix = jax.scipy.linalg.solve_triangular(lower_factor, matrix.T, lower=True).T
    return matrix


def subspace(operator_gram, initial, sweeps):
    current = initial
    for repeat in range(sweeps):
        current = orthonormal(jnp.dot(operator_gram, current, precision=HIGHEST))
    return current


class Torus:
    def __init__(self):
        self.blk = lax.axis_size("blk")
        self.side = {"x": lax.axis_size("pen")}
        self.side["y"] = 4
        self.side["z"] = self.blk // 8
        index = lax.axis_index("blk")
        self.core = index % 2
        self.place = {"x": lax.axis_index("pen"), "y": (index // 2) % 4, "z": index // 8}

    def swap(self, value, axis, step):
        if axis == "x":
            return lax.ppermute(value, "pen", [(s, s ^ step) for s in range(self.side["x"])])
        step = {"core": step, "y": step * 2, "z": step * 8}[axis]
        return lax.ppermute(value, "blk", [(s, s ^ step) for s in range(self.blk)])

    def all_sum(self, value, axis):
        near, across, far = [self.swap(value, axis, step) for step in (1, 2, 3)]
        return (value + near) + (across + far)

    def scatter_sum(self, value, axis):
        pieces = value.reshape((4, value.shape[0] // 4) + value.shape[1:])
        place = self.place[axis]
        take = lambda step: lax.dynamic_index_in_dim(pieces, place ^ step, 0, False)
        near, across, far = [self.swap(take(step), axis, step) for step in (1, 2, 3)]
        return (take(0) + near) + (across + far)

    def gather(self, value, axis):
        place = self.place[axis]
        result = jnp.zeros((4,) + value.shape, value.dtype)
        for step in range(4):
            piece = value if step == 0 else self.swap(value, axis, step)
            result = lax.dynamic_update_index_in_dim(result, piece, place ^ step, 0)
        return result.reshape((4 * value.shape[0],) + value.shape[1:])

    def core_scatter_sum(self, value):
        pieces = value.reshape((2, value.shape[0] // 2) + value.shape[1:])
        mine = lax.dynamic_index_in_dim(pieces, self.core, 0, False)
        other = lax.dynamic_index_in_dim(pieces, 1 - self.core, 0, False)
        return mine + self.swap(other, "core", 1)

    def core_gather(self, value):
        other = self.swap(value, "core", 1)
        first = jnp.where(self.core == 0, value, other)
        second = jnp.where(self.core == 0, other, value)
        return jnp.concatenate([first, second])


def on_device(snapshots, start_time, start_plane):
    variables, planes, cell_count, window = snapshots.shape
    devices_all = lax.axis_size("blk") * lax.axis_size("pen")
    torus = Torus()
    row_matrix = snapshots.reshape(variables * planes * cell_count, window)
    partial_time = jnp.dot(row_matrix.T, row_matrix, preferred_element_type=jnp.float32)
    total_time = torus.core_scatter_sum(partial_time)
    for axis in "xyz":
        total_time = torus.all_sum(total_time, axis)
    total_time = torus.core_gather(total_time)
    gram_time = total_time / float(variables * planes * cell_count * devices_all)
    time_basis = subspace(gram_time, start_time, ITT)
    time_narrow = time_basis.astype(jnp.bfloat16)
    zero_block = jnp.zeros_like(time_narrow)
    pair_basis = jnp.stack(
        [
            jnp.concatenate([time_narrow, zero_block], axis=1),
            jnp.concatenate([zero_block, time_narrow], axis=1),
        ]
    )
    pair_count = cell_count // 2
    paired = snapshots.reshape(variables, planes, pair_count, 2, window)
    core_time = jnp.einsum(
        "vxpqt,qtl->vxpl", paired, pair_basis, preferred_element_type=jnp.float32
    ).astype(jnp.bfloat16)
    pencils = lax.all_to_all(core_time, ("blk", "pen"), split_axis=2, concat_axis=1, tiled=True)
    column_total = float(variables * pencils.shape[2] * pencils.shape[3] * devices_all)
    partial_plane = jnp.einsum(
        "vxpl,vypl->xy", pencils, pencils, preferred_element_type=jnp.float32
    )
    total_plane = torus.core_scatter_sum(partial_plane)
    total_plane = torus.scatter_sum(total_plane, "x")
    total_plane = torus.all_sum(total_plane, "y")
    total_plane = torus.all_sum(total_plane, "z")
    total_plane = torus.core_gather(torus.gather(total_plane, "x"))
    gram_plane = total_plane / column_total
    plane_basis = subspace(gram_plane, start_plane, ITX)
    plane_narrow = plane_basis.astype(jnp.bfloat16)
    core_blocks = jnp.einsum(
        "xk,vxpl->vkpl", plane_narrow, pencils, preferred_element_type=jnp.float32
    ).astype(jnp.bfloat16)
    core_tensor = core_blocks.reshape(variables, core_blocks.shape[1], -1)
    return (time_basis, plane_basis, core_tensor)


def solution(mesh):
    return jax.shard_map(
        on_device,
        mesh=mesh,
        in_specs=(P(None, ("blk", "pen"), None, None), P(), P()),
        out_specs=(P(), P(), P(None, None, ("blk", "pen"))),
        check_vma=False,
    )
```

```python
import jax
import jax.numpy as jnp
from jax import lax
from jax.experimental import pallas as pl
from jax.experimental.pallas import tpu as pltpu
from jax.sharding import PartitionSpec as P

ITT = 3
ITX = 3

F32, BF16 = jnp.float32, jnp.bfloat16
HIGHEST = lax.Precision.HIGHEST
VMEM = pl.BlockSpec(memory_space=pltpu.VMEM)


class Torus:
    def __init__(self):
        self.blk = lax.axis_size("blk")
        self.pen = lax.axis_size("pen")
        index = lax.axis_index("blk")
        self.core = index % 2
        self.place = {"x": lax.axis_index("pen"), "y": (index // 2) % 4, "z": index // 8}

    def swap(self, value, axis, step):
        if axis == "x":
            return lax.ppermute(value, "pen", [(s, s ^ step) for s in range(self.pen)])
        step = {"core": step, "y": step * 2, "z": step * 8}[axis]
        return lax.ppermute(value, "blk", [(s, s ^ step) for s in range(self.blk)])

    def all_sum(self, value, axis):
        near, across, far = [self.swap(value, axis, step) for step in (1, 2, 3)]
        return (value + near) + (across + far)

    def scatter_sum(self, value, axis):
        pieces = value.reshape((4, value.shape[0] // 4) + value.shape[1:])
        place = self.place[axis]
        take = lambda step: lax.dynamic_index_in_dim(pieces, place ^ step, 0, False)
        near, across, far = [self.swap(take(step), axis, step) for step in (1, 2, 3)]
        return (take(0) + near) + (across + far)

    def gather(self, value, axis):
        place = self.place[axis]
        result = jnp.zeros((4,) + value.shape, value.dtype)
        for step in range(4):
            piece = value if step == 0 else self.swap(value, axis, step)
            result = lax.dynamic_update_index_in_dim(result, piece, place ^ step, 0)
        return result.reshape((4 * value.shape[0],) + value.shape[1:])

    def core_scatter_sum(self, value):
        pieces = value.reshape((2, value.shape[0] // 2) + value.shape[1:])
        mine = lax.dynamic_index_in_dim(pieces, self.core, 0, False)
        other = lax.dynamic_index_in_dim(pieces, 1 - self.core, 0, False)
        return mine + self.swap(other, "core", 1)

    def core_gather(self, value):
        other = self.swap(value, "core", 1)
        first = jnp.where(self.core == 0, value, other)
        second = jnp.where(self.core == 0, other, value)
        return jnp.concatenate([first, second])


def product(a, b, dim_a, dim_b, precision=HIGHEST):
    dims = (((dim_a,), (dim_b,)), ((), ()))
    return lax.dot_general(a, b, dims, precision=precision, preferred_element_type=F32)


def narrow_product(a, b, dim_a, dim_b):
    return product(a, b, dim_a, dim_b, None)


def identity(size):
    shape = (size, size)
    same = lax.broadcasted_iota(jnp.int32, shape, 0) == lax.broadcasted_iota(jnp.int32, shape, 1)
    return jnp.where(same, 1.0, 0.0).astype(F32)


def inverse_factor(square):
    size = square.shape[0]
    width = 2 * size
    wide = jnp.concatenate([square, identity(size)], axis=1)
    rows = [wide[8 * i : 8 * i + 8] for i in range(size // 8)]
    place = lax.broadcasted_iota(jnp.int32, (8, 1), 0)
    for block in range(size // 8):
        held = rows[block]
        splats = [
            jnp.broadcast_to(held[:, 8 * block + j : 8 * block + j + 1], (8, width)) for j in range(8)
        ]
        for j in range(8):
            factor = jnp.where(place > j, splats[j] * (1.0 / splats[j][j : j + 1]), 0.0)
            held = held - factor * held[j : j + 1]
            for m in range(j + 1, 8):
                splats[m] = splats[m] - factor * splats[m][j : j + 1]
        pivots = jnp.concatenate([splats[j][j : j + 1] for j in range(8)], axis=0)
        held = held * lax.rsqrt(pivots)
        rows[block] = held
        for i in range(block + 1, size // 8):
            column = held[:, 8 * i : 8 * i + 8].T
            total = rows[i]
            for j in range(8):
                total = total - column[:, j : j + 1] * held[j : j + 1]
            rows[i] = total
    return jnp.concatenate(rows, axis=0)[:, size:]


def subspace(gram, flat, sweeps):
    for sweep in range(sweeps):
        flat = product(flat, gram, 1, 0)
        for repeat in range(2 if sweep == sweeps - 1 else 1):
            flat = product(inverse_factor(product(flat, flat, 1, 1)), flat, 1, 0)
    return flat


def time_gram(snapshots):
    variables, planes, cells, window = snapshots.shape
    half = variables // 2
    steps = planes * half

    def kernel(low_ref, high_ref, out_ref, total):
        step = pl.program_id(0) * half + pl.program_id(1)
        both = jnp.concatenate([low_ref[0, 0], high_ref[0, 0]], axis=1)
        part = narrow_product(both, both, 0, 0)

        @pl.when(step == 0)
        def _():
            total[...] = part

        @pl.when(step > 0)
        def _():
            total[...] += part

        @pl.when(step == steps - 1)
        def _():
            out_ref[...] = total[:window, :window] + total[window:, window:]

    block = (1, 1, cells, window)
    return pl.pallas_call(
        kernel,
        grid=(planes, half),
        in_specs=[
            pl.BlockSpec(block, lambda x, v: (v, x, 0, 0)),
            pl.BlockSpec(block, lambda x, v: (v + half, x, 0, 0)),
        ],
        out_specs=pl.BlockSpec((window, window), lambda x, v: (0, 0)),
        out_shape=jax.ShapeDtypeStruct((window, window), F32),
        scratch_shapes=[pltpu.VMEM((2 * window, 2 * window), F32)],
    )(snapshots, snapshots)


def time_subspace(total, start, scale):
    rank, window = start.shape

    def kernel(gram_ref, start_ref, basis_ref, pair_ref):
        flat = subspace(gram_ref[...] * scale, start_ref[...], ITT)
        basis_ref[...] = flat
        narrow = flat.T.astype(BF16)
        zero = jnp.zeros_like(narrow)
        pair_ref[:window] = jnp.concatenate([narrow, zero], axis=1)
        pair_ref[window:] = jnp.concatenate([zero, narrow], axis=1)

    return pl.pallas_call(
        kernel,
        in_specs=[VMEM, VMEM],
        out_specs=[VMEM, VMEM],
        out_shape=[
            jax.ShapeDtypeStruct((rank, window), F32),
            jax.ShapeDtypeStruct((2 * window, 2 * rank), BF16),
        ],
    )(total, start)


def truncate_time(snapshots, pair_basis, owners):
    variables, planes, cells, window = snapshots.shape
    half = variables // 2
    lanes = pair_basis.shape[1]
    mine = cells // owners

    def kernel(low_ref, high_ref, basis_ref, out_ref):
        both = jnp.concatenate([low_ref[0, 0], high_ref[0, 0]], axis=1)
        core = narrow_product(both, basis_ref[...], 1, 0).astype(BF16)
        out_ref[...] = core.reshape(owners, 1, 1, mine, lanes)

    block = (1, 1, cells, window)
    return pl.pallas_call(
        kernel,
        grid=(planes, half),
        in_specs=[
            pl.BlockSpec(block, lambda x, v: (v, x, 0, 0)),
            pl.BlockSpec(block, lambda x, v: (v + half, x, 0, 0)),
            pl.BlockSpec(pair_basis.shape, lambda x, v: (0, 0)),
        ],
        out_specs=pl.BlockSpec((owners, 1, 1, mine, lanes), lambda x, v: (0, x, v, 0, 0)),
        out_shape=jax.ShapeDtypeStruct((owners, planes, half, mine, lanes), BF16),
    )(snapshots, snapshots, pair_basis)


def plane_gram(pencils):
    planes, groups, lanes = pencils.shape
    taken = 16

    def kernel(pencil_ref, gram_ref, group_ref):
        step = pl.program_id(0)
        turned = jnp.swapaxes(pencil_ref[...], 0, 1)
        group_ref[...] = turned
        total = None
        for j in range(0, taken, 2):
            both = jnp.concatenate([turned[j], turned[j + 1]], axis=1)
            part = narrow_product(both, both, 1, 1)
            total = part if total is None else total + part

        @pl.when(step == 0)
        def _():
            gram_ref[...] = total

        @pl.when(step > 0)
        def _():
            gram_ref[...] += total

    return pl.pallas_call(
        kernel,
        grid=(groups // taken,),
        in_specs=[pl.BlockSpec((planes, taken, lanes), lambda i: (0, i, 0))],
        out_specs=[
            pl.BlockSpec((planes, planes), lambda i: (0, 0)),
            pl.BlockSpec((taken, planes, lanes), lambda i: (i, 0, 0)),
        ],
        out_shape=[
            jax.ShapeDtypeStruct((planes, planes), F32),
            jax.ShapeDtypeStruct((groups, planes, lanes), BF16),
        ],
    )(pencils)


def plane_subspace(total, start, groups, scale, half):
    rank, planes = start.shape
    count, _, lanes = groups.shape
    mine = count // half
    ranks = lanes // 2

    def kernel(gram_ref, start_ref, groups_ref, basis_ref, core_ref, held, arrived):
        fetch = pltpu.make_async_copy(groups_ref, held, arrived)
        fetch.start()
        flat = subspace(gram_ref[...] * scale, start_ref[...], ITX)
        basis_ref[...] = flat
        narrow = flat.astype(BF16)
        fetch.wait()
        first = lax.broadcasted_iota(jnp.int32, (rank, lanes), 1) < ranks
        for v in range(half):
            for pair in range(mine // 2):
                even = narrow_product(narrow, held[v * mine + 2 * pair], 1, 0)
                odd = narrow_product(narrow, held[v * mine + 2 * pair + 1], 1, 0)
                low = jnp.where(first, even, pltpu.roll(odd, ranks, 1))
                high = jnp.where(first, pltpu.roll(even, ranks, 1), odd)
                place = slice(pair * lanes, (pair + 1) * lanes)
                core_ref[v, :, place] = low.astype(BF16)
                core_ref[v + half, :, place] = high.astype(BF16)

    return pl.pallas_call(
        kernel,
        in_specs=[VMEM, VMEM, pl.BlockSpec(memory_space=pl.ANY)],
        out_specs=[VMEM, VMEM],
        out_shape=[
            jax.ShapeDtypeStruct((rank, planes), F32),
            jax.ShapeDtypeStruct((2 * half, rank, mine * ranks), BF16),
        ],
        scratch_shapes=[pltpu.VMEM(groups.shape, BF16), pltpu.SemaphoreType.DMA],
    )(total, start, groups)


def on_device(snapshots, start_time, start_plane):
    variables, planes, cells, window = snapshots.shape
    devices_all = lax.axis_size("blk") * lax.axis_size("pen")
    half = variables // 2
    rank = start_time.shape[1]
    torus = Torus()

    total_time = torus.core_scatter_sum(time_gram(snapshots))
    for axis in "xyz":
        total_time = torus.all_sum(total_time, axis)
    total_time = torus.core_gather(total_time)
    scale_time = 1.0 / float(variables * planes * cells * devices_all)
    time_basis, pair_basis = time_subspace(total_time, start_time.T, scale_time)

    core_time = truncate_time(snapshots, pair_basis, devices_all)
    pencils = lax.all_to_all(core_time, ("blk", "pen"), split_axis=0, concat_axis=0, tiled=True)
    partial_plane, groups = plane_gram(pencils.reshape(devices_all * planes, -1, 2 * rank))

    total_plane = torus.core_scatter_sum(partial_plane)
    total_plane = torus.scatter_sum(total_plane, "x")
    total_plane = torus.all_sum(total_plane, "y")
    total_plane = torus.all_sum(total_plane, "z")
    total_plane = torus.core_gather(torus.gather(total_plane, "x"))
    scale_plane = 1.0 / float(variables * cells * rank)
    plane_basis, core_tensor = plane_subspace(total_plane, start_plane.T, groups, scale_plane, half)
    return (time_basis.T, plane_basis.T, core_tensor)


def solution(mesh):
    return jax.shard_map(
        on_device,
        mesh=mesh,
        in_specs=(P(None, ("blk", "pen"), None, None), P(), P()),
        out_specs=(P(), P(), P(None, None, ("blk", "pen"))),
        check_vma=False,
    )
```

```python
import jax
import jax.numpy as jnp
from jax import lax
from jax.experimental import pallas as pl
from jax.experimental.pallas import tpu as pltpu
from jax.sharding import PartitionSpec as P

ITT = 3
ITX = 3

F32, BF16 = jnp.float32, jnp.bfloat16
HIGHEST = lax.Precision.HIGHEST
VMEM = pl.BlockSpec(memory_space=pltpu.VMEM)
SMEM = pl.BlockSpec(memory_space=pltpu.SMEM)
HBM = pl.BlockSpec(memory_space=pltpu.HBM)


class Torus:
    def __init__(self):
        self.blk = lax.axis_size("blk")
        self.pen = lax.axis_size("pen")
        index = lax.axis_index("blk")
        self.core = index % 2
        self.place = {"x": lax.axis_index("pen"), "y": (index // 2) % 4, "z": index // 8}

    def swap(self, value, axis, step):
        if axis == "x":
            return lax.ppermute(value, "pen", [(s, s ^ step) for s in range(self.pen)])
        step = {"core": step, "y": step * 2, "z": step * 8}[axis]
        return lax.ppermute(value, "blk", [(s, s ^ step) for s in range(self.blk)])

    def all_sum(self, value, axis):
        near, across, far = [self.swap(value, axis, step) for step in (1, 2, 3)]
        return (value + near) + (across + far)

    def scatter_sum(self, value, axis):
        pieces = value.reshape((4, value.shape[0] // 4) + value.shape[1:])
        place = self.place[axis]
        take = lambda step: lax.dynamic_index_in_dim(pieces, place ^ step, 0, False)
        near, across, far = [self.swap(take(step), axis, step) for step in (1, 2, 3)]
        return (take(0) + near) + (across + far)

    def gather(self, value, axis):
        place = self.place[axis]
        result = jnp.zeros((4,) + value.shape, value.dtype)
        for step in range(4):
            piece = value if step == 0 else self.swap(value, axis, step)
            result = lax.dynamic_update_index_in_dim(result, piece, place ^ step, 0)
        return result.reshape((4 * value.shape[0],) + value.shape[1:])


def limit(mebibytes):
    return pltpu.CompilerParams(vmem_limit_bytes=mebibytes << 20)


def product(a, b, dim_a, dim_b, precision=HIGHEST):
    dims = (((dim_a,), (dim_b,)), ((), ()))
    return lax.dot_general(a, b, dims, precision=precision, preferred_element_type=F32)


def narrow_product(a, b, dim_a, dim_b):
    return product(a, b, dim_a, dim_b, None)


def identity(size):
    shape = (size, size)
    same = lax.broadcasted_iota(jnp.int32, shape, 0) == lax.broadcasted_iota(jnp.int32, shape, 1)
    return jnp.where(same, 1.0, 0.0).astype(F32)


def inverse_factor(square):
    size = square.shape[0]
    width = 2 * size
    wide = jnp.concatenate([square, identity(size)], axis=1)
    rows = [wide[8 * i : 8 * i + 8] for i in range(size // 8)]
    place = lax.broadcasted_iota(jnp.int32, (8, 1), 0)
    for block in range(size // 8):
        held = rows[block]
        splats = [
            jnp.broadcast_to(held[:, 8 * block + j : 8 * block + j + 1], (8, width)) for j in range(8)
        ]
        for j in range(8):
            factor = jnp.where(place > j, splats[j] * (1.0 / splats[j][j : j + 1]), 0.0)
            held = held - factor * held[j : j + 1]
            for m in range(j + 1, 8):
                splats[m] = splats[m] - factor * splats[m][j : j + 1]
        pivots = jnp.concatenate([splats[j][j : j + 1] for j in range(8)], axis=0)
        held = held * lax.rsqrt(pivots)
        rows[block] = held
        for i in range(block + 1, size // 8):
            column = held[:, 8 * i : 8 * i + 8].T
            total = rows[i]
            for j in range(8):
                total = total - column[:, j : j + 1] * held[j : j + 1]
            rows[i] = total
    return jnp.concatenate(rows, axis=0)[:, size:]


def subspace(gram, flat, sweeps):
    for sweep in range(sweeps):
        flat = product(flat, gram, 1, 0)
        for repeat in range(2 if sweep == sweeps - 1 else 1):
            flat = product(inverse_factor(product(flat, flat, 1, 1)), flat, 1, 0)
    return flat


def time_gram(core, snapshots):
    variables, planes, cells, window = snapshots.shape
    pieces = 8
    rows = variables * planes * cells // pieces

    def kernel(core_ref, far_ref, mine_ref, other_ref, near_ref, arrived):
        fetches = []
        for i in range(pieces):
            place = pl.ds(i * rows, rows)
            fetches.append(
                pltpu.make_async_copy(far_ref.at[place], near_ref.at[place], arrived.at[i])
            )
            fetches[-1].start()
        total = None
        for i in range(pieces):
            fetches[i].wait()
            first, second = [
                near_ref[i * rows + j * rows // 2 : i * rows + (j + 1) * rows // 2] for j in range(2)
            ]
            both = jnp.concatenate([first, second], axis=1)
            part = narrow_product(both, both, 0, 0)
            total = part if total is None else total + part
        total = total[:window, :window] + total[window:, window:]
        split_halves(core_ref, total, mine_ref, other_ref)

    half = jax.ShapeDtypeStruct((window // 2, window), F32)
    return pl.pallas_call(
        kernel,
        in_specs=[SMEM, HBM],
        out_specs=[VMEM, VMEM, VMEM],
        out_shape=[half, half, pltpu.VMEM((pieces * rows, window), BF16)],
        scratch_shapes=[pltpu.SemaphoreType.DMA((pieces,))],
        compiler_params=limit(24),
    )(core, pltpu.with_memory_space_constraint(snapshots.reshape(pieces * rows, window), pltpu.HBM))


def split_halves(core_ref, total, mine_ref, other_ref):
    first = core_ref[0] == 0
    rows = total.shape[0] // 2
    mine_ref[...] = jnp.where(first, total[:rows], total[rows:])
    other_ref[...] = jnp.where(first, total[rows:], total[:rows])


def join_halves(core_ref, mine_ref, other_ref, scale):
    first = core_ref[0] == 0
    mine, other = mine_ref[...] * scale, other_ref[...] * scale
    return jnp.concatenate([jnp.where(first, mine, other), jnp.where(first, other, mine)])


def time_subspace(core, mine, other, start, scale):
    rank, window = start.shape

    def kernel(core_ref, mine_ref, other_ref, start_ref, basis_ref, pair_ref):
        gram = join_halves(core_ref, mine_ref, other_ref, scale)
        flat = subspace(gram, start_ref[...], ITT)
        basis_ref[...] = flat
        narrow = flat.T.astype(BF16)
        zero = jnp.zeros_like(narrow)
        pair_ref[:window] = jnp.concatenate([narrow, zero], axis=1)
        pair_ref[window:] = jnp.concatenate([zero, narrow], axis=1)

    return pl.pallas_call(
        kernel,
        in_specs=[SMEM, VMEM, VMEM, VMEM],
        out_specs=[VMEM, VMEM],
        out_shape=[
            jax.ShapeDtypeStruct((rank, window), F32),
            jax.ShapeDtypeStruct((2 * window, 2 * rank), BF16),
        ],
        compiler_params=limit(6),
    )(core, mine, other, start)


def truncate_time(shape, near, pair_basis, owners):
    variables, planes, cells, window = shape
    half = variables // 2
    lanes = pair_basis.shape[1]
    own = cells // owners

    def kernel(near_ref, basis_ref, out_ref):
        basis = basis_ref[...]
        for v in range(half):
            for x in range(planes):
                low, high = [((v + side) * planes + x) * cells for side in (0, half)]
                both = jnp.concatenate(
                    [near_ref[low : low + cells], near_ref[high : high + cells]], axis=1
                )
                core = narrow_product(both, basis, 1, 0).astype(BF16)
                out_ref[:, x, v] = core.reshape(owners, own, lanes)

    return pl.pallas_call(
        kernel,
        in_specs=[VMEM, VMEM],
        out_specs=VMEM,
        out_shape=jax.ShapeDtypeStruct((owners, planes, half, own, lanes), BF16),
        compiler_params=limit(24),
    )(pltpu.with_memory_space_constraint(near, pltpu.VMEM), pair_basis)


def plane_gram(core, pencils):
    planes, groups, lanes = pencils.shape

    def kernel(core_ref, pencil_ref, mine_ref, other_ref, group_ref, held, sent):
        total, sends = None, []
        for i in range(0, groups, 16):
            turned = jnp.swapaxes(pencil_ref[:, i : i + 16], 0, 1)
            place = pl.ds(i, 16)
            held[place] = turned
            sends.append(pltpu.make_async_copy(held.at[place], group_ref.at[place], sent.at[i // 16]))
            sends[-1].start()
            for j in range(0, 16, 2):
                both = jnp.concatenate([turned[j], turned[j + 1]], axis=1)
                part = narrow_product(both, both, 1, 1)
                total = part if total is None else total + part
        split_halves(core_ref, total, mine_ref, other_ref)
        for send in sends:
            send.wait()

    half = jax.ShapeDtypeStruct((planes // 2, planes), F32)
    return pl.pallas_call(
        kernel,
        in_specs=[SMEM, VMEM],
        out_specs=[VMEM, VMEM, HBM],
        out_shape=[half, half, pltpu.HBM((groups, planes, lanes), BF16)],
        scratch_shapes=[
            pltpu.VMEM((groups, planes, lanes), BF16),
            pltpu.SemaphoreType.DMA((groups // 16,)),
        ],
        compiler_params=limit(24),
    )(core, pencils)


def plane_subspace(core, mine, other, start, groups, scale, half):
    rank, planes = start.shape
    count, _, lanes = groups.shape
    own = count // half
    ranks = lanes // 2

    def kernel(core_ref, mine_ref, other_ref, start_ref, far_ref, basis_ref, out_ref, group_ref, arrived):
        fetch = pltpu.make_async_copy(far_ref, group_ref, arrived)
        fetch.start()
        gram = join_halves(core_ref, mine_ref, other_ref, scale)
        flat = subspace(gram, start_ref[...], ITX)
        basis_ref[...] = flat
        narrow = flat.astype(BF16)
        fetch.wait()
        first = lax.broadcasted_iota(jnp.int32, (rank, lanes), 1) < ranks
        for v in range(half):
            for pair in range(own // 2):
                even = narrow_product(narrow, group_ref[v * own + 2 * pair], 1, 0)
                odd = narrow_product(narrow, group_ref[v * own + 2 * pair + 1], 1, 0)
                low = jnp.where(first, even, pltpu.roll(odd, ranks, 1))
                high = jnp.where(first, pltpu.roll(even, ranks, 1), odd)
                place = slice(pair * lanes, (pair + 1) * lanes)
                out_ref[v, :, place] = low.astype(BF16)
                out_ref[v + half, :, place] = high.astype(BF16)

    return pl.pallas_call(
        kernel,
        in_specs=[SMEM, VMEM, VMEM, VMEM, HBM],
        out_specs=[VMEM, VMEM],
        out_shape=[
            jax.ShapeDtypeStruct((rank, planes), F32),
            jax.ShapeDtypeStruct((2 * half, rank, own * ranks), BF16),
        ],
        scratch_shapes=[pltpu.VMEM(groups.shape, BF16), pltpu.SemaphoreType.DMA],
        compiler_params=limit(16),
    )(core, mine, other, start, pltpu.with_memory_space_constraint(groups, pltpu.HBM))


def on_device(snapshots, start_time, start_plane):
    variables, planes, cells, window = snapshots.shape
    devices_all = lax.axis_size("blk") * lax.axis_size("pen")
    half = variables // 2
    rank = start_time.shape[1]
    torus = Torus()
    core = torus.core.reshape(1)

    mine, other, near = time_gram(core, snapshots)
    total = mine + torus.swap(other, "core", 1)
    for axis in "xyz":
        total = torus.all_sum(total, axis)
    scale_time = 1.0 / float(variables * planes * cells * devices_all)
    time_basis, pair_basis = time_subspace(
        core, total, torus.swap(total, "core", 1), start_time.T, scale_time
    )

    core_time = truncate_time(snapshots.shape, near, pair_basis, devices_all)
    pencils = lax.all_to_all(core_time, ("blk", "pen"), split_axis=0, concat_axis=0, tiled=True)
    mine, other, groups = plane_gram(core, pencils.reshape(devices_all * planes, -1, 2 * rank))

    total = mine + torus.swap(other, "core", 1)
    total = torus.scatter_sum(total, "x")
    total = torus.all_sum(total, "y")
    total = torus.all_sum(total, "z")
    total = torus.gather(total, "x")
    scale_plane = 1.0 / float(variables * cells * rank)
    plane_basis, core_tensor = plane_subspace(
        core, total, torus.swap(total, "core", 1), start_plane.T, groups, scale_plane, half
    )
    return (time_basis.T, plane_basis.T, core_tensor)


def solution(mesh):
    return jax.shard_map(
        on_device,
        mesh=mesh,
        in_specs=(P(None, ("blk", "pen"), None, None), P(), P()),
        out_specs=(P(), P(), P(None, None, ("blk", "pen"))),
        check_vma=False,
    )
```

```python
import jax
import jax.numpy as jnp
from jax import lax
from jax.experimental import pallas as pl
from jax.experimental.pallas import tpu as pltpu
from jax.sharding import PartitionSpec as P

ITT = 3
ITX = 3

F32, BF16 = jnp.float32, jnp.bfloat16
HIGHEST = lax.Precision.HIGHEST
VMEM = pl.BlockSpec(memory_space=pltpu.VMEM)
SMEM = pl.BlockSpec(memory_space=pltpu.SMEM)
HBM = pl.BlockSpec(memory_space=pltpu.HBM)


class Torus:
    def __init__(self):
        self.blk = lax.axis_size("blk")
        self.pen = lax.axis_size("pen")
        index = lax.axis_index("blk")
        self.core = index % 2
        self.place = {"x": lax.axis_index("pen"), "y": (index // 2) % 4, "z": index // 8}

    def swap(self, value, axis, step):
        if axis == "x":
            return lax.ppermute(value, "pen", [(s, s ^ step) for s in range(self.pen)])
        step = {"core": step, "y": step * 2, "z": step * 8}[axis]
        return lax.ppermute(value, "blk", [(s, s ^ step) for s in range(self.blk)])

    def all_sum(self, value, axis):
        near, across, far = [self.swap(value, axis, step) for step in (1, 2, 3)]
        return (value + near) + (across + far)

    def scatter_sum(self, value, axis):
        pieces = value.reshape((4, value.shape[0] // 4) + value.shape[1:])
        place = self.place[axis]
        take = lambda step: lax.dynamic_index_in_dim(pieces, place ^ step, 0, False)
        near, across, far = [self.swap(take(step), axis, step) for step in (1, 2, 3)]
        return (take(0) + near) + (across + far)

    def gather(self, value, axis):
        place = self.place[axis]
        result = jnp.zeros((4,) + value.shape, value.dtype)
        for step in range(4):
            piece = value if step == 0 else self.swap(value, axis, step)
            result = lax.dynamic_update_index_in_dim(result, piece, place ^ step, 0)
        return result.reshape((4 * value.shape[0],) + value.shape[1:])


def limit(mebibytes):
    return pltpu.CompilerParams(vmem_limit_bytes=mebibytes << 20)


def product(a, b, dim_a, dim_b, precision=HIGHEST):
    dims = (((dim_a,), (dim_b,)), ((), ()))
    return lax.dot_general(a, b, dims, precision=precision, preferred_element_type=F32)


def narrow_product(a, b, dim_a, dim_b):
    return product(a, b, dim_a, dim_b, None)


def identity(size):
    shape = (size, size)
    same = lax.broadcasted_iota(jnp.int32, shape, 0) == lax.broadcasted_iota(jnp.int32, shape, 1)
    return jnp.where(same, 1.0, 0.0).astype(F32)


def inverse_factor(square):
    size = square.shape[0]
    blocks = size // 8
    wide = jnp.concatenate([square, identity(size)], axis=1)
    rows = [wide[8 * i : 8 * i + 8] for i in range(blocks)]
    place = lax.broadcasted_iota(jnp.int32, (8, 1), 0)
    for block in range(blocks):
        columns = slice(8 * block, 8 * block + 8)
        splats = {
            i: [jnp.broadcast_to(rows[i][:, columns][:, j : j + 1], wide[:8].shape) for j in range(8)]
            for i in range(block, blocks)
        }
        pivots = splats[block]
        done = []
        for j in range(8):
            root = lax.rsqrt(pivots[j][j : j + 1])
            scaled = rows[block][j : j + 1] * root
            factors = {i: splats[i][j] * root for i in splats}
            factors[block] = jnp.where(place > j, factors[block], 0.0)
            pivot_row = {m: pivots[m][j : j + 1] * root for m in range(j + 1, 8)}
            for i in splats:
                rows[i] = rows[i] - factors[i] * scaled
                for m in pivot_row:
                    splats[i][m] = splats[i][m] - factors[i] * pivot_row[m]
            done.append(scaled)
        rows[block] = jnp.concatenate(done, axis=0)
    return jnp.concatenate(rows, axis=0)[:, size:]


def subspace(gram, flat, sweeps):
    for sweep in range(sweeps):
        flat = product(flat, gram, 1, 0)
        for repeat in range(2 if sweep == sweeps - 1 else 1):
            flat = product(inverse_factor(product(flat, flat, 1, 1)), flat, 1, 0)
    return flat


def time_gram(core, snapshots):
    variables, planes, cells, window = snapshots.shape
    pieces = 8
    rows = variables * planes * cells // pieces

    def kernel(core_ref, far_ref, mine_ref, other_ref, near_ref, arrived):
        fetches = []
        for i in range(pieces):
            place = pl.ds(i * rows, rows)
            fetches.append(
                pltpu.make_async_copy(far_ref.at[place], near_ref.at[place], arrived.at[i])
            )
            fetches[-1].start()
        total = None
        for i in range(pieces):
            fetches[i].wait()
            first, second = [
                near_ref[i * rows + j * rows // 2 : i * rows + (j + 1) * rows // 2] for j in range(2)
            ]
            both = jnp.concatenate([first, second], axis=1)
            part = narrow_product(both, both, 0, 0)
            total = part if total is None else total + part
        total = total[:window, :window] + total[window:, window:]
        split_halves(core_ref, total, mine_ref, other_ref)

    half = jax.ShapeDtypeStruct((window // 2, window), F32)
    return pl.pallas_call(
        kernel,
        in_specs=[SMEM, HBM],
        out_specs=[VMEM, VMEM, VMEM],
        out_shape=[half, half, pltpu.VMEM((pieces * rows, window), BF16)],
        scratch_shapes=[pltpu.SemaphoreType.DMA((pieces,))],
        compiler_params=limit(24),
    )(core, pltpu.with_memory_space_constraint(snapshots.reshape(pieces * rows, window), pltpu.HBM))


def split_halves(core_ref, total, mine_ref, other_ref):
    first = core_ref[0] == 0
    rows = total.shape[0] // 2
    mine_ref[...] = jnp.where(first, total[:rows], total[rows:])
    other_ref[...] = jnp.where(first, total[rows:], total[:rows])


def join_halves(core_ref, mine_ref, other_ref, scale):
    first = core_ref[0] == 0
    mine, other = mine_ref[...] * scale, other_ref[...] * scale
    return jnp.concatenate([jnp.where(first, mine, other), jnp.where(first, other, mine)])


def time_subspace(core, mine, other, start, scale):
    rank, window = start.shape

    def kernel(core_ref, mine_ref, other_ref, start_ref, basis_ref, pair_ref):
        gram = join_halves(core_ref, mine_ref, other_ref, scale)
        flat = subspace(gram, start_ref[...], ITT)
        basis_ref[...] = flat
        narrow = flat.T.astype(BF16)
        zero = jnp.zeros_like(narrow)
        pair_ref[:window] = jnp.concatenate([narrow, zero], axis=1)
        pair_ref[window:] = jnp.concatenate([zero, narrow], axis=1)

    return pl.pallas_call(
        kernel,
        in_specs=[SMEM, VMEM, VMEM, VMEM],
        out_specs=[VMEM, VMEM],
        out_shape=[
            jax.ShapeDtypeStruct((rank, window), F32),
            jax.ShapeDtypeStruct((2 * window, 2 * rank), BF16),
        ],
        compiler_params=limit(6),
    )(core, mine, other, start)


def truncate_time(shape, near, pair_basis, owners):
    variables, planes, cells, window = shape
    half = variables // 2
    lanes = pair_basis.shape[1]
    own = cells // owners

    def kernel(near_ref, basis_ref, out_ref):
        basis = basis_ref[...]
        for v in range(half):
            for x in range(planes):
                low, high = [((v + side) * planes + x) * cells for side in (0, half)]
                both = jnp.concatenate(
                    [near_ref[low : low + cells], near_ref[high : high + cells]], axis=1
                )
                core = narrow_product(both, basis, 1, 0).astype(BF16)
                out_ref[:, x, v] = core.reshape(owners, own, lanes)

    return pl.pallas_call(
        kernel,
        in_specs=[VMEM, VMEM],
        out_specs=VMEM,
        out_shape=jax.ShapeDtypeStruct((owners, planes, half, own, lanes), BF16),
        compiler_params=limit(24),
    )(pltpu.with_memory_space_constraint(near, pltpu.VMEM), pair_basis)


def plane_gram(core, pencils):
    planes, groups, lanes = pencils.shape

    def kernel(core_ref, pencil_ref, mine_ref, other_ref, group_ref, held, sent):
        total, sends = None, []
        for i in range(0, groups, 16):
            turned = jnp.swapaxes(pencil_ref[:, i : i + 16], 0, 1)
            place = pl.ds(i, 16)
            held[place] = turned
            sends.append(pltpu.make_async_copy(held.at[place], group_ref.at[place], sent.at[i // 16]))
            sends[-1].start()
            for j in range(0, 16, 2):
                both = jnp.concatenate([turned[j], turned[j + 1]], axis=1)
                part = narrow_product(both, both, 1, 1)
                total = part if total is None else total + part
        split_halves(core_ref, total, mine_ref, other_ref)
        for send in sends:
            send.wait()

    half = jax.ShapeDtypeStruct((planes // 2, planes), F32)
    return pl.pallas_call(
        kernel,
        in_specs=[SMEM, VMEM],
        out_specs=[VMEM, VMEM, HBM],
        out_shape=[half, half, pltpu.HBM((groups, planes, lanes), BF16)],
        scratch_shapes=[
            pltpu.VMEM((groups, planes, lanes), BF16),
            pltpu.SemaphoreType.DMA((groups // 16,)),
        ],
        compiler_params=limit(24),
    )(core, pencils)


def plane_subspace(core, mine, other, start, groups, scale, half):
    rank, planes = start.shape
    count, _, lanes = groups.shape
    own = count // half
    ranks = lanes // 2

    def kernel(core_ref, mine_ref, other_ref, start_ref, far_ref, basis_ref, out_ref, group_ref, arrived):
        fetch = pltpu.make_async_copy(far_ref, group_ref, arrived)
        fetch.start()
        gram = join_halves(core_ref, mine_ref, other_ref, scale)
        flat = subspace(gram, start_ref[...], ITX)
        basis_ref[...] = flat
        narrow = flat.astype(BF16)
        fetch.wait()
        first = lax.broadcasted_iota(jnp.int32, (rank, lanes), 1) < ranks
        for v in range(half):
            for pair in range(own // 2):
                even = narrow_product(narrow, group_ref[v * own + 2 * pair], 1, 0)
                odd = narrow_product(narrow, group_ref[v * own + 2 * pair + 1], 1, 0)
                low = jnp.where(first, even, pltpu.roll(odd, ranks, 1))
                high = jnp.where(first, pltpu.roll(even, ranks, 1), odd)
                place = slice(pair * lanes, (pair + 1) * lanes)
                out_ref[v, :, place] = low.astype(BF16)
                out_ref[v + half, :, place] = high.astype(BF16)

    return pl.pallas_call(
        kernel,
        in_specs=[SMEM, VMEM, VMEM, VMEM, HBM],
        out_specs=[VMEM, VMEM],
        out_shape=[
            jax.ShapeDtypeStruct((rank, planes), F32),
            jax.ShapeDtypeStruct((2 * half, rank, own * ranks), BF16),
        ],
        scratch_shapes=[pltpu.VMEM(groups.shape, BF16), pltpu.SemaphoreType.DMA],
        compiler_params=limit(16),
    )(core, mine, other, start, pltpu.with_memory_space_constraint(groups, pltpu.HBM))


def on_device(snapshots, start_time, start_plane):
    variables, planes, cells, window = snapshots.shape
    devices_all = lax.axis_size("blk") * lax.axis_size("pen")
    half = variables // 2
    rank = start_time.shape[1]
    torus = Torus()
    core = torus.core.reshape(1)

    mine, other, near = time_gram(core, snapshots)
    total = mine + torus.swap(other, "core", 1)
    for axis in "xyz":
        total = torus.all_sum(total, axis)
    scale_time = 1.0 / float(variables * planes * cells * devices_all)
    time_basis, pair_basis = time_subspace(
        core, total, torus.swap(total, "core", 1), start_time.T, scale_time
    )

    core_time = truncate_time(snapshots.shape, near, pair_basis, devices_all)
    pencils = lax.all_to_all(core_time, ("blk", "pen"), split_axis=0, concat_axis=0, tiled=True)
    mine, other, groups = plane_gram(core, pencils.reshape(devices_all * planes, -1, 2 * rank))

    total = mine + torus.swap(other, "core", 1)
    total = torus.scatter_sum(total, "x")
    total = torus.all_sum(total, "y")
    total = torus.all_sum(total, "z")
    total = torus.gather(total, "x")
    scale_plane = 1.0 / float(variables * cells * rank)
    plane_basis, core_tensor = plane_subspace(
        core, total, torus.swap(total, "core", 1), start_plane.T, groups, scale_plane, half
    )
    return (time_basis.T, plane_basis.T, core_tensor)


def solution(mesh):
    return jax.shard_map(
        on_device,
        mesh=mesh,
        in_specs=(P(None, ("blk", "pen"), None, None), P(), P()),
        out_specs=(P(), P(), P(None, None, ("blk", "pen"))),
        check_vma=False,
    )
```

```python
import jax
import jax.numpy as jnp
from jax import lax
from jax.experimental import pallas as pl
from jax.experimental.pallas import tpu as pltpu
from jax.sharding import PartitionSpec as P

ITT = 3
ITX = 3

F32, BF16 = jnp.float32, jnp.bfloat16
HIGHEST = lax.Precision.HIGHEST
VMEM = pl.BlockSpec(memory_space=pltpu.VMEM)
SMEM = pl.BlockSpec(memory_space=pltpu.SMEM)
HBM = pl.BlockSpec(memory_space=pltpu.HBM)


class Torus:
    orders = ("xyz", "yzx")
    steps = (2, 3, 1)

    def __init__(self):
        self.blk = lax.axis_size("blk")
        self.pen = lax.axis_size("pen")
        index = lax.axis_index("blk")
        self.core = index % 2
        self.place = {"x": lax.axis_index("pen"), "y": (index // 2) % 4, "z": index // 8}

    def partners(self, stage, step):
        pairs = []
        for blk in range(self.blk):
            axis = "core" if stage is None else self.orders[blk % 2][stage]
            for pen in range(self.pen):
                to_pen = pen ^ step if axis == "x" else pen
                to_blk = blk ^ (step * {"core": 1, "x": 0, "y": 2, "z": 8}[axis])
                pairs.append((blk * self.pen + pen, to_blk * self.pen + to_pen))
        return pairs

    def swap(self, value, stage, step):
        return lax.ppermute(value, ("blk", "pen"), self.partners(stage, step))

    def swap_cores(self, value):
        return self.swap(value, None, 1)

    def stage_place(self, stage):
        first, second = [self.place[order[stage]] for order in self.orders]
        return jnp.where(self.core == 0, first, second)

    def all_sum(self, value, stage):
        got = {step: self.swap(value, stage, step) for step in self.steps}
        return (value + got[1]) + (got[2] + got[3])

    def scatter_sum(self, value, stage):
        pieces = value.reshape((4, value.shape[0] // 4) + value.shape[1:])
        place = self.stage_place(stage)
        take = lambda step: lax.dynamic_index_in_dim(pieces, place ^ step, 0, False)
        got = {step: self.swap(take(step), stage, step) for step in self.steps}
        return (take(0) + got[1]) + (got[2] + got[3])

    def gather(self, value, stage):
        place = self.stage_place(stage)
        result = jnp.zeros((4,) + value.shape, value.dtype)
        for step in (0,) + self.steps:
            piece = value if step == 0 else self.swap(value, stage, step)
            result = lax.dynamic_update_index_in_dim(result, piece, place ^ step, 0)
        return result.reshape((4 * value.shape[0],) + value.shape[1:])


def limit(mebibytes):
    return pltpu.CompilerParams(vmem_limit_bytes=mebibytes << 20)


def product(a, b, dim_a, dim_b, precision=HIGHEST):
    dims = (((dim_a,), (dim_b,)), ((), ()))
    return lax.dot_general(a, b, dims, precision=precision, preferred_element_type=F32)


def narrow_product(a, b, dim_a, dim_b):
    return product(a, b, dim_a, dim_b, None)


def identity(size):
    shape = (size, size)
    same = lax.broadcasted_iota(jnp.int32, shape, 0) == lax.broadcasted_iota(jnp.int32, shape, 1)
    return jnp.where(same, 1.0, 0.0).astype(F32)


def inverse_factor(square):
    size = square.shape[0]
    blocks = size // 8
    wide = jnp.concatenate([square, identity(size)], axis=1)
    rows = [wide[8 * i : 8 * i + 8] for i in range(blocks)]
    place = lax.broadcasted_iota(jnp.int32, (8, 1), 0)
    for block in range(blocks):
        columns = slice(8 * block, 8 * block + 8)
        splats = {
            i: [jnp.broadcast_to(rows[i][:, columns][:, j : j + 1], wide[:8].shape) for j in range(8)]
            for i in range(block, blocks)
        }
        pivots = splats[block]
        done = []
        for j in range(8):
            root = lax.rsqrt(pivots[j][j : j + 1])
            scaled = rows[block][j : j + 1] * root
            factors = {i: splats[i][j] * root for i in splats}
            factors[block] = jnp.where(place > j, factors[block], 0.0)
            pivot_row = {m: pivots[m][j : j + 1] * root for m in range(j + 1, 8)}
            for i in splats:
                rows[i] = rows[i] - factors[i] * scaled
                for m in pivot_row:
                    splats[i][m] = splats[i][m] - factors[i] * pivot_row[m]
            done.append(scaled)
        rows[block] = jnp.concatenate(done, axis=0)
    return jnp.concatenate(rows, axis=0)[:, size:]


def subspace(gram, flat, sweeps):
    for sweep in range(sweeps):
        flat = product(flat, gram, 1, 0)
        for repeat in range(2 if sweep == sweeps - 1 else 1):
            flat = product(inverse_factor(product(flat, flat, 1, 1)), flat, 1, 0)
    return flat


def time_gram(core, snapshots):
    variables, planes, cells, window = snapshots.shape
    pieces = 8
    rows = variables * planes * cells // pieces

    def kernel(core_ref, far_ref, mine_ref, other_ref, near_ref, arrived):
        fetches = []
        for i in range(pieces):
            place = pl.ds(i * rows, rows)
            fetches.append(
                pltpu.make_async_copy(far_ref.at[place], near_ref.at[place], arrived.at[i])
            )
            fetches[-1].start()
        total = None
        for i in range(pieces):
            fetches[i].wait()
            first, second = [
                near_ref[i * rows + j * rows // 2 : i * rows + (j + 1) * rows // 2] for j in range(2)
            ]
            both = jnp.concatenate([first, second], axis=1)
            part = narrow_product(both, both, 0, 0)
            total = part if total is None else total + part
        total = total[:window, :window] + total[window:, window:]
        split_halves(core_ref, total, mine_ref, other_ref)

    half = jax.ShapeDtypeStruct((window // 2, window), F32)
    return pl.pallas_call(
        kernel,
        in_specs=[SMEM, HBM],
        out_specs=[VMEM, VMEM, VMEM],
        out_shape=[half, half, pltpu.VMEM((pieces * rows, window), BF16)],
        scratch_shapes=[pltpu.SemaphoreType.DMA((pieces,))],
        compiler_params=limit(24),
    )(core, pltpu.with_memory_space_constraint(snapshots.reshape(pieces * rows, window), pltpu.HBM))


def split_halves(core_ref, total, mine_ref, other_ref):
    first = core_ref[0] == 0
    rows = total.shape[0] // 2
    mine_ref[...] = jnp.where(first, total[:rows], total[rows:])
    other_ref[...] = jnp.where(first, total[rows:], total[:rows])


def join_halves(core_ref, mine_ref, other_ref, scale):
    first = core_ref[0] == 0
    mine, other = mine_ref[...] * scale, other_ref[...] * scale
    return jnp.concatenate([jnp.where(first, mine, other), jnp.where(first, other, mine)])


def time_subspace(core, mine, other, start, scale):
    rank, window = start.shape

    def kernel(core_ref, mine_ref, other_ref, start_ref, basis_ref, pair_ref):
        gram = join_halves(core_ref, mine_ref, other_ref, scale)
        flat = subspace(gram, start_ref[...], ITT)
        basis_ref[...] = flat
        narrow = flat.T.astype(BF16)
        zero = jnp.zeros_like(narrow)
        pair_ref[:window] = jnp.concatenate([narrow, zero], axis=1)
        pair_ref[window:] = jnp.concatenate([zero, narrow], axis=1)

    return pl.pallas_call(
        kernel,
        in_specs=[SMEM, VMEM, VMEM, VMEM],
        out_specs=[VMEM, VMEM],
        out_shape=[
            jax.ShapeDtypeStruct((rank, window), F32),
            jax.ShapeDtypeStruct((2 * window, 2 * rank), BF16),
        ],
        compiler_params=limit(6),
    )(core, mine, other, start)


def truncate_time(shape, near, pair_basis, owners):
    variables, planes, cells, window = shape
    half = variables // 2
    lanes = pair_basis.shape[1]
    own = cells // owners

    def kernel(near_ref, basis_ref, out_ref):
        basis = basis_ref[...]
        for v in range(half):
            for x in range(planes):
                low, high = [((v + side) * planes + x) * cells for side in (0, half)]
                both = jnp.concatenate(
                    [near_ref[low : low + cells], near_ref[high : high + cells]], axis=1
                )
                core = narrow_product(both, basis, 1, 0).astype(BF16)
                out_ref[:, x, v] = core.reshape(owners, own, lanes)

    return pl.pallas_call(
        kernel,
        in_specs=[VMEM, VMEM],
        out_specs=VMEM,
        out_shape=jax.ShapeDtypeStruct((owners, planes, half, own, lanes), BF16),
        compiler_params=limit(24),
    )(pltpu.with_memory_space_constraint(near, pltpu.VMEM), pair_basis)


def plane_gram(core, pencils):
    planes, groups, lanes = pencils.shape

    def kernel(core_ref, pencil_ref, mine_ref, other_ref, group_ref, held, sent):
        total, sends = None, []
        for i in range(0, groups, 16):
            turned = jnp.swapaxes(pencil_ref[:, i : i + 16], 0, 1)
            place = pl.ds(i, 16)
            held[place] = turned
            sends.append(pltpu.make_async_copy(held.at[place], group_ref.at[place], sent.at[i // 16]))
            sends[-1].start()
            for j in range(0, 16, 2):
                both = jnp.concatenate([turned[j], turned[j + 1]], axis=1)
                part = narrow_product(both, both, 1, 1)
                total = part if total is None else total + part
        split_halves(core_ref, total, mine_ref, other_ref)
        for send in sends:
            send.wait()

    half = jax.ShapeDtypeStruct((planes // 2, planes), F32)
    return pl.pallas_call(
        kernel,
        in_specs=[SMEM, VMEM],
        out_specs=[VMEM, VMEM, HBM],
        out_shape=[half, half, pltpu.HBM((groups, planes, lanes), BF16)],
        scratch_shapes=[
            pltpu.VMEM((groups, planes, lanes), BF16),
            pltpu.SemaphoreType.DMA((groups // 16,)),
        ],
        compiler_params=limit(24),
    )(core, pencils)


def plane_subspace(core, mine, other, start, groups, scale, half):
    rank, planes = start.shape
    count, _, lanes = groups.shape
    own = count // half
    ranks = lanes // 2

    def kernel(core_ref, mine_ref, other_ref, start_ref, far_ref, basis_ref, out_ref, group_ref, arrived):
        fetch = pltpu.make_async_copy(far_ref, group_ref, arrived)
        fetch.start()
        gram = join_halves(core_ref, mine_ref, other_ref, scale)
        flat = subspace(gram, start_ref[...], ITX)
        basis_ref[...] = flat
        narrow = flat.astype(BF16)
        fetch.wait()
        first = lax.broadcasted_iota(jnp.int32, (rank, lanes), 1) < ranks
        for v in range(half):
            for pair in range(own // 2):
                even = narrow_product(narrow, group_ref[v * own + 2 * pair], 1, 0)
                odd = narrow_product(narrow, group_ref[v * own + 2 * pair + 1], 1, 0)
                low = jnp.where(first, even, pltpu.roll(odd, ranks, 1))
                high = jnp.where(first, pltpu.roll(even, ranks, 1), odd)
                place = slice(pair * lanes, (pair + 1) * lanes)
                out_ref[v, :, place] = low.astype(BF16)
                out_ref[v + half, :, place] = high.astype(BF16)

    return pl.pallas_call(
        kernel,
        in_specs=[SMEM, VMEM, VMEM, VMEM, HBM],
        out_specs=[VMEM, VMEM],
        out_shape=[
            jax.ShapeDtypeStruct((rank, planes), F32),
            jax.ShapeDtypeStruct((2 * half, rank, own * ranks), BF16),
        ],
        scratch_shapes=[pltpu.VMEM(groups.shape, BF16), pltpu.SemaphoreType.DMA],
        compiler_params=limit(16),
    )(core, mine, other, start, pltpu.with_memory_space_constraint(groups, pltpu.HBM))


def on_device(snapshots, start_time, start_plane):
    variables, planes, cells, window = snapshots.shape
    devices_all = lax.axis_size("blk") * lax.axis_size("pen")
    half = variables // 2
    rank = start_time.shape[1]
    torus = Torus()
    core = torus.core.reshape(1)

    mine, other, near = time_gram(core, snapshots)
    total = mine + torus.swap_cores(other)
    for stage in range(3):
        total = torus.all_sum(total, stage)
    scale_time = 1.0 / float(variables * planes * cells * devices_all)
    time_basis, pair_basis = time_subspace(
        core, total, torus.swap_cores(total), start_time.T, scale_time
    )

    core_time = truncate_time(snapshots.shape, near, pair_basis, devices_all)
    pencils = lax.all_to_all(core_time, ("blk", "pen"), split_axis=0, concat_axis=0, tiled=True)
    mine, other, groups = plane_gram(core, pencils.reshape(devices_all * planes, -1, 2 * rank))

    total = mine + torus.swap_cores(other)
    total = torus.scatter_sum(total, 0)
    for stage in (1, 2):
        total = torus.all_sum(total, stage)
    total = torus.gather(total, 0)
    scale_plane = 1.0 / float(variables * cells * rank)
    plane_basis, core_tensor = plane_subspace(
        core, total, torus.swap_cores(total), start_plane.T, groups, scale_plane, half
    )
    return (time_basis.T, plane_basis.T, core_tensor)


def solution(mesh):
    return jax.shard_map(
        on_device,
        mesh=mesh,
        in_specs=(P(None, ("blk", "pen"), None, None), P(), P()),
        out_specs=(P(), P(), P(None, None, ("blk", "pen"))),
        check_vma=False,
    )
```

```python
import jax
import jax.numpy as jnp
from jax import lax
from jax.experimental import pallas as pl
from jax.experimental.pallas import tpu as pltpu
from jax.sharding import PartitionSpec as P

ITT = 3
ITX = 3

F32, BF16 = jnp.float32, jnp.bfloat16
PIVOT_FLOOR = 1e-5
HIGHEST = lax.Precision.HIGHEST
VMEM = pl.BlockSpec(memory_space=pltpu.VMEM)
SMEM = pl.BlockSpec(memory_space=pltpu.SMEM)
HBM = pl.BlockSpec(memory_space=pltpu.HBM)


class Torus:
    orders = ("xyz", "yzx")
    steps = (2, 3, 1)

    def __init__(self):
        self.blk = lax.axis_size("blk")
        self.pen = lax.axis_size("pen")
        index = lax.axis_index("blk")
        self.core = index % 2
        self.place = {"x": lax.axis_index("pen"), "y": (index // 2) % 4, "z": index // 8}

    def partners(self, stage, step):
        pairs = []
        for blk in range(self.blk):
            axis = "core" if stage is None else self.orders[blk % 2][stage]
            for pen in range(self.pen):
                to_pen = pen ^ step if axis == "x" else pen
                to_blk = blk ^ (step * {"core": 1, "x": 0, "y": 2, "z": 8}[axis])
                pairs.append((blk * self.pen + pen, to_blk * self.pen + to_pen))
        return pairs

    def swap(self, value, stage, step):
        return lax.ppermute(value, ("blk", "pen"), self.partners(stage, step))

    def swap_cores(self, value):
        return self.swap(value, None, 1)

    def stage_place(self, stage):
        first, second = [self.place[order[stage]] for order in self.orders]
        return jnp.where(self.core == 0, first, second)

    def all_sum(self, value, stage):
        got = {step: self.swap(value, stage, step) for step in self.steps}
        return (value + got[1]) + (got[2] + got[3])

    def scatter_sum(self, value, stage):
        pieces = value.reshape((4, value.shape[0] // 4) + value.shape[1:])
        place = self.stage_place(stage)
        take = lambda step: lax.dynamic_index_in_dim(pieces, place ^ step, 0, False)
        got = {step: self.swap(take(step), stage, step) for step in self.steps}
        return (take(0) + got[1]) + (got[2] + got[3])

    def gather(self, value, stage):
        place = self.stage_place(stage)
        result = jnp.zeros((4,) + value.shape, value.dtype)
        for step in (0,) + self.steps:
            piece = value if step == 0 else self.swap(value, stage, step)
            result = lax.dynamic_update_index_in_dim(result, piece, place ^ step, 0)
        return result.reshape((4 * value.shape[0],) + value.shape[1:])


def limit(mebibytes):
    return pltpu.CompilerParams(vmem_limit_bytes=mebibytes << 20)


def product(a, b, dim_a, dim_b, precision=HIGHEST):
    dims = (((dim_a,), (dim_b,)), ((), ()))
    return lax.dot_general(a, b, dims, precision=precision, preferred_element_type=F32)


def narrow_product(a, b, dim_a, dim_b):
    return product(a, b, dim_a, dim_b, None)


def identity(size):
    shape = (size, size)
    same = lax.broadcasted_iota(jnp.int32, shape, 0) == lax.broadcasted_iota(jnp.int32, shape, 1)
    return jnp.where(same, 1.0, 0.0).astype(F32)


def inverse_factor(square):
    size = square.shape[0]
    blocks = size // 8
    wide = jnp.concatenate([square, identity(size)], axis=1)
    rows = [wide[8 * i : 8 * i + 8] for i in range(blocks)]
    place = lax.broadcasted_iota(jnp.int32, (8, 1), 0)
    for block in range(blocks):
        columns = slice(8 * block, 8 * block + 8)
        splats = {
            i: [jnp.broadcast_to(rows[i][:, columns][:, j : j + 1], wide[:8].shape) for j in range(8)]
            for i in range(block, blocks)
        }
        pivots = splats[block]
        done = []
        for j in range(8):
            root = lax.rsqrt(pivots[j][j : j + 1])
            scaled = rows[block][j : j + 1] * root
            factors = {i: splats[i][j] * root for i in splats}
            factors[block] = jnp.where(place > j, factors[block], 0.0)
            pivot_row = {m: pivots[m][j : j + 1] * root for m in range(j + 1, 8)}
            for i in splats:
                rows[i] = rows[i] - factors[i] * scaled
                for m in pivot_row:
                    splats[i][m] = splats[i][m] - factors[i] * pivot_row[m]
            done.append(scaled)
        rows[block] = jnp.concatenate(done, axis=0)
    return jnp.concatenate(rows, axis=0)[:, size:]


def orthonormal_round(flat):
    square = product(flat, flat, 1, 1)
    inverse = inverse_factor(square)
    same = identity(square.shape[0])
    lead = jnp.sum(inverse * same, axis=1, keepdims=True)
    diagonal = jnp.sum(square * same, axis=1, keepdims=True)
    weak = jnp.where(lead * lead * diagonal * PIVOT_FLOOR < 1.0, 0.0, 1.0)
    return product(inverse, flat, 1, 0), jnp.sum(weak)


def separate_sweeps(gram, start, sweeps):
    flat = start
    for sweep in range(sweeps):
        flat = orthonormal_round(product(flat, gram, 1, 0))[0]
    return orthonormal_round(flat)[0]


def joined_sweeps(gram_ref, start, sweeps, flat_ref):
    gram = gram_ref[...]
    flat = start
    for sweep in range(sweeps - 2):
        flat = orthonormal_round(product(flat, gram, 1, 0))[0]
    flat = product(product(flat, gram, 1, 0), gram, 1, 0)
    flat, weak = orthonormal_round(flat)
    flat_ref[...] = orthonormal_round(flat)[0]

    @pl.when(weak > 0.0)
    def _():
        flat_ref[...] = start

        @pl.loop(0, sweeps + 1)
        def _(index):
            @pl.when(index < sweeps)
            def _():
                flat_ref[...] = product(flat_ref[...], gram_ref[...], 1, 0)

            flat_ref[...] = orthonormal_round(flat_ref[...])[0]


def time_gram(core, snapshots):
    variables, planes, cells, window = snapshots.shape
    pieces = 8
    rows = variables * planes * cells // pieces

    def kernel(core_ref, far_ref, mine_ref, other_ref, near_ref, arrived):
        fetches = []
        for i in range(pieces):
            place = pl.ds(i * rows, rows)
            fetches.append(
                pltpu.make_async_copy(far_ref.at[place], near_ref.at[place], arrived.at[i])
            )
            fetches[-1].start()
        total = None
        for i in range(pieces):
            fetches[i].wait()
            first, second = [
                near_ref[i * rows + j * rows // 2 : i * rows + (j + 1) * rows // 2] for j in range(2)
            ]
            both = jnp.concatenate([first, second], axis=1)
            part = narrow_product(both, both, 0, 0)
            total = part if total is None else total + part
        total = total[:window, :window] + total[window:, window:]
        split_halves(core_ref, total, mine_ref, other_ref)

    half = jax.ShapeDtypeStruct((window // 2, window), F32)
    return pl.pallas_call(
        kernel,
        in_specs=[SMEM, HBM],
        out_specs=[VMEM, VMEM, VMEM],
        out_shape=[half, half, pltpu.VMEM((pieces * rows, window), BF16)],
        scratch_shapes=[pltpu.SemaphoreType.DMA((pieces,))],
        compiler_params=limit(24),
    )(core, pltpu.with_memory_space_constraint(snapshots.reshape(pieces * rows, window), pltpu.HBM))


def split_halves(core_ref, total, mine_ref, other_ref):
    first = core_ref[0] == 0
    rows = total.shape[0] // 2
    mine_ref[...] = jnp.where(first, total[:rows], total[rows:])
    other_ref[...] = jnp.where(first, total[rows:], total[:rows])


def join_halves(core_ref, mine_ref, other_ref, scale):
    first = core_ref[0] == 0
    mine, other = mine_ref[...] * scale, other_ref[...] * scale
    return jnp.concatenate([jnp.where(first, mine, other), jnp.where(first, other, mine)])


def time_subspace(core, mine, other, start, scale):
    rank, window = start.shape

    def kernel(core_ref, mine_ref, other_ref, start_ref, basis_ref, pair_ref, held_ref):
        held_ref[...] = join_halves(core_ref, mine_ref, other_ref, scale)
        joined_sweeps(held_ref, start_ref[...], ITT, basis_ref)
        narrow = basis_ref[...].T.astype(BF16)
        zero = jnp.zeros_like(narrow)
        pair_ref[:window] = jnp.concatenate([narrow, zero], axis=1)
        pair_ref[window:] = jnp.concatenate([zero, narrow], axis=1)

    return pl.pallas_call(
        kernel,
        in_specs=[SMEM, VMEM, VMEM, VMEM],
        out_specs=[VMEM, VMEM],
        out_shape=[
            jax.ShapeDtypeStruct((rank, window), F32),
            jax.ShapeDtypeStruct((2 * window, 2 * rank), BF16),
        ],
        scratch_shapes=[pltpu.VMEM((window, window), F32)],
        compiler_params=limit(6),
    )(core, mine, other, start)


def truncate_time(shape, near, pair_basis, owners):
    variables, planes, cells, window = shape
    half = variables // 2
    lanes = pair_basis.shape[1]
    own = cells // owners

    def kernel(near_ref, basis_ref, out_ref):
        basis = basis_ref[...]
        for v in range(half):
            for x in range(planes):
                low, high = [((v + side) * planes + x) * cells for side in (0, half)]
                both = jnp.concatenate(
                    [near_ref[low : low + cells], near_ref[high : high + cells]], axis=1
                )
                core = narrow_product(both, basis, 1, 0).astype(BF16)
                out_ref[:, x, v] = core.reshape(owners, own, lanes)

    return pl.pallas_call(
        kernel,
        in_specs=[VMEM, VMEM],
        out_specs=VMEM,
        out_shape=jax.ShapeDtypeStruct((owners, planes, half, own, lanes), BF16),
        compiler_params=limit(24),
    )(pltpu.with_memory_space_constraint(near, pltpu.VMEM), pair_basis)


def plane_gram(core, pencils):
    planes, groups, lanes = pencils.shape

    def kernel(core_ref, pencil_ref, mine_ref, other_ref, group_ref, held, sent):
        total, sends = None, []
        for i in range(0, groups, 16):
            turned = jnp.swapaxes(pencil_ref[:, i : i + 16], 0, 1)
            place = pl.ds(i, 16)
            held[place] = turned
            sends.append(pltpu.make_async_copy(held.at[place], group_ref.at[place], sent.at[i // 16]))
            sends[-1].start()
            for j in range(0, 16, 2):
                both = jnp.concatenate([turned[j], turned[j + 1]], axis=1)
                part = narrow_product(both, both, 1, 1)
                total = part if total is None else total + part
        split_halves(core_ref, total, mine_ref, other_ref)
        for send in sends:
            send.wait()

    half = jax.ShapeDtypeStruct((planes // 2, planes), F32)
    return pl.pallas_call(
        kernel,
        in_specs=[SMEM, VMEM],
        out_specs=[VMEM, VMEM, HBM],
        out_shape=[half, half, pltpu.HBM((groups, planes, lanes), BF16)],
        scratch_shapes=[
            pltpu.VMEM((groups, planes, lanes), BF16),
            pltpu.SemaphoreType.DMA((groups // 16,)),
        ],
        compiler_params=limit(24),
    )(core, pencils)


def plane_subspace(core, mine, other, start, groups, scale, half):
    rank, planes = start.shape
    count, _, lanes = groups.shape
    own = count // half
    ranks = lanes // 2

    def kernel(core_ref, mine_ref, other_ref, start_ref, far_ref, basis_ref, out_ref, group_ref, arrived):
        fetch = pltpu.make_async_copy(far_ref, group_ref, arrived)
        fetch.start()
        gram = join_halves(core_ref, mine_ref, other_ref, scale)
        flat = separate_sweeps(gram, start_ref[...], ITX)
        basis_ref[...] = flat
        narrow = flat.astype(BF16)
        fetch.wait()
        first = lax.broadcasted_iota(jnp.int32, (rank, lanes), 1) < ranks
        for v in range(half):
            for pair in range(own // 2):
                even = narrow_product(narrow, group_ref[v * own + 2 * pair], 1, 0)
                odd = narrow_product(narrow, group_ref[v * own + 2 * pair + 1], 1, 0)
                low = jnp.where(first, even, pltpu.roll(odd, ranks, 1))
                high = jnp.where(first, pltpu.roll(even, ranks, 1), odd)
                place = slice(pair * lanes, (pair + 1) * lanes)
                out_ref[v, :, place] = low.astype(BF16)
                out_ref[v + half, :, place] = high.astype(BF16)

    return pl.pallas_call(
        kernel,
        in_specs=[SMEM, VMEM, VMEM, VMEM, HBM],
        out_specs=[VMEM, VMEM],
        out_shape=[
            jax.ShapeDtypeStruct((rank, planes), F32),
            jax.ShapeDtypeStruct((2 * half, rank, own * ranks), BF16),
        ],
        scratch_shapes=[pltpu.VMEM(groups.shape, BF16), pltpu.SemaphoreType.DMA],
        compiler_params=limit(16),
    )(core, mine, other, start, pltpu.with_memory_space_constraint(groups, pltpu.HBM))


def on_device(snapshots, start_time, start_plane):
    variables, planes, cells, window = snapshots.shape
    devices_all = lax.axis_size("blk") * lax.axis_size("pen")
    half = variables // 2
    rank = start_time.shape[1]
    torus = Torus()
    core = torus.core.reshape(1)

    mine, other, near = time_gram(core, snapshots)
    total = mine + torus.swap_cores(other)
    for stage in range(3):
        total = torus.all_sum(total, stage)
    scale_time = 1.0 / float(variables * planes * cells * devices_all)
    time_basis, pair_basis = time_subspace(
        core, total, torus.swap_cores(total), start_time.T, scale_time
    )

    core_time = truncate_time(snapshots.shape, near, pair_basis, devices_all)
    pencils = lax.all_to_all(core_time, ("blk", "pen"), split_axis=0, concat_axis=0, tiled=True)
    mine, other, groups = plane_gram(core, pencils.reshape(devices_all * planes, -1, 2 * rank))

    total = mine + torus.swap_cores(other)
    total = torus.scatter_sum(total, 0)
    for stage in (1, 2):
        total = torus.all_sum(total, stage)
    total = torus.gather(total, 0)
    scale_plane = 1.0 / float(variables * cells * rank)
    plane_basis, core_tensor = plane_subspace(
        core, total, torus.swap_cores(total), start_plane.T, groups, scale_plane, half
    )
    return (time_basis.T, plane_basis.T, core_tensor)


def solution(mesh):
    return jax.shard_map(
        on_device,
        mesh=mesh,
        in_specs=(P(None, ("blk", "pen"), None, None), P(), P()),
        out_specs=(P(), P(), P(None, None, ("blk", "pen"))),
        check_vma=False,
    )
```

```python
import jax
import jax.numpy as jnp
from jax import lax
from jax.experimental import pallas as pl
from jax.experimental.pallas import tpu as pltpu
from jax.sharding import PartitionSpec as P

ITT = 3
ITX = 3

F32, BF16 = jnp.float32, jnp.bfloat16
PIVOT_FLOOR = 1e-5
HIGHEST = lax.Precision.HIGHEST
VMEM = pl.BlockSpec(memory_space=pltpu.VMEM)
SMEM = pl.BlockSpec(memory_space=pltpu.SMEM)
HBM = pl.BlockSpec(memory_space=pltpu.HBM)


class Torus:
    orders = ("xyz", "yzx")
    steps = (2, 3, 1)

    def __init__(self):
        self.blk = lax.axis_size("blk")
        self.pen = lax.axis_size("pen")
        index = lax.axis_index("blk")
        self.core = index % 2
        self.place = {"x": lax.axis_index("pen"), "y": (index // 2) % 4, "z": index // 8}

    def partners(self, stage, step):
        pairs = []
        for blk in range(self.blk):
            axis = "core" if stage is None else self.orders[blk % 2][stage]
            for pen in range(self.pen):
                to_pen = pen ^ step if axis == "x" else pen
                to_blk = blk ^ (step * {"core": 1, "x": 0, "y": 2, "z": 8}[axis])
                pairs.append((blk * self.pen + pen, to_blk * self.pen + to_pen))
        return pairs

    def swap(self, value, stage, step):
        return lax.ppermute(value, ("blk", "pen"), self.partners(stage, step))

    def swap_cores(self, value):
        return self.swap(value, None, 1)

    def stage_place(self, stage):
        first, second = [self.place[order[stage]] for order in self.orders]
        return jnp.where(self.core == 0, first, second)

    def all_sum(self, value, stage):
        got = {step: self.swap(value, stage, step) for step in self.steps}
        return (value + got[1]) + (got[2] + got[3])

    def scatter_sum(self, value, stage):
        pieces = value.reshape((4, value.shape[0] // 4) + value.shape[1:])
        place = self.stage_place(stage)
        take = lambda step: lax.dynamic_index_in_dim(pieces, place ^ step, 0, False)
        got = {step: self.swap(take(step), stage, step) for step in self.steps}
        return (take(0) + got[1]) + (got[2] + got[3])

    def gather(self, value, stage):
        place = self.stage_place(stage)
        result = jnp.zeros((4,) + value.shape, value.dtype)
        for step in (0,) + self.steps:
            piece = value if step == 0 else self.swap(value, stage, step)
            result = lax.dynamic_update_index_in_dim(result, piece, place ^ step, 0)
        return result.reshape((4 * value.shape[0],) + value.shape[1:])


def limit(mebibytes):
    return pltpu.CompilerParams(vmem_limit_bytes=mebibytes << 20)


def product(a, b, dim_a, dim_b, precision=HIGHEST):
    dims = (((dim_a,), (dim_b,)), ((), ()))
    return lax.dot_general(a, b, dims, precision=precision, preferred_element_type=F32)


def narrow_product(a, b, dim_a, dim_b):
    return product(a, b, dim_a, dim_b, None)


def identity(size):
    shape = (size, size)
    same = lax.broadcasted_iota(jnp.int32, shape, 0) == lax.broadcasted_iota(jnp.int32, shape, 1)
    return jnp.where(same, 1.0, 0.0).astype(F32)


def inverse_factor(square):
    size = square.shape[0]
    blocks = size // 8
    wide = jnp.concatenate([square, identity(size)], axis=1)
    rows = [wide[8 * i : 8 * i + 8] for i in range(blocks)]
    place = lax.broadcasted_iota(jnp.int32, (8, 1), 0)
    for block in range(blocks):
        columns = slice(8 * block, 8 * block + 8)
        splats = {
            i: [jnp.broadcast_to(rows[i][:, columns][:, j : j + 1], wide[:8].shape) for j in range(8)]
            for i in range(block, blocks)
        }
        pivots = splats[block]
        done = []
        for j in range(8):
            root = lax.rsqrt(pivots[j][j : j + 1])
            scaled = rows[block][j : j + 1] * root
            factors = {i: splats[i][j] * root for i in splats}
            factors[block] = jnp.where(place > j, factors[block], 0.0)
            pivot_row = {m: pivots[m][j : j + 1] * root for m in range(j + 1, 8)}
            for i in splats:
                rows[i] = rows[i] - factors[i] * scaled
                for m in pivot_row:
                    splats[i][m] = splats[i][m] - factors[i] * pivot_row[m]
            done.append(scaled)
        rows[block] = jnp.concatenate(done, axis=0)
    return jnp.concatenate(rows, axis=0)[:, size:]


def orthonormal_round(flat):
    square = product(flat, flat, 1, 1)
    inverse = inverse_factor(square)
    same = identity(square.shape[0])
    lead = jnp.sum(inverse * same, axis=1, keepdims=True)
    diagonal = jnp.sum(square * same, axis=1, keepdims=True)
    weak = jnp.where(lead * lead * diagonal * PIVOT_FLOOR < 1.0, 0.0, 1.0)
    return product(inverse, flat, 1, 0), jnp.sum(weak)


def joined_sweeps(gram_ref, start, sweeps, flat_ref):
    gram = gram_ref[...]
    flat = start
    for sweep in range(sweeps - 2):
        flat = orthonormal_round(product(flat, gram, 1, 0))[0]
    flat = product(product(flat, gram, 1, 0), gram, 1, 0)
    flat, weak = orthonormal_round(flat)
    flat_ref[...] = orthonormal_round(flat)[0]

    @pl.when(weak > 0.0)
    def _():
        flat_ref[...] = start

        @pl.loop(0, sweeps + 1)
        def _(index):
            @pl.when(index < sweeps)
            def _():
                flat_ref[...] = product(flat_ref[...], gram_ref[...], 1, 0)

            flat_ref[...] = orthonormal_round(flat_ref[...])[0]


def time_gram(core, snapshots):
    variables, planes, cells, window = snapshots.shape
    pieces = 8
    rows = variables * planes * cells // pieces

    def kernel(core_ref, far_ref, mine_ref, other_ref, near_ref, arrived):
        fetches = []
        for i in range(pieces):
            place = pl.ds(i * rows, rows)
            fetches.append(
                pltpu.make_async_copy(far_ref.at[place], near_ref.at[place], arrived.at[i])
            )
            fetches[-1].start()
        total = None
        for i in range(pieces):
            fetches[i].wait()
            first, second = [
                near_ref[i * rows + j * rows // 2 : i * rows + (j + 1) * rows // 2] for j in range(2)
            ]
            both = jnp.concatenate([first, second], axis=1)
            part = narrow_product(both, both, 0, 0)
            total = part if total is None else total + part
        total = total[:window, :window] + total[window:, window:]
        split_halves(core_ref, total, mine_ref, other_ref)

    half = jax.ShapeDtypeStruct((window // 2, window), F32)
    return pl.pallas_call(
        kernel,
        in_specs=[SMEM, HBM],
        out_specs=[VMEM, VMEM, VMEM],
        out_shape=[half, half, pltpu.VMEM((pieces * rows, window), BF16)],
        scratch_shapes=[pltpu.SemaphoreType.DMA((pieces,))],
        compiler_params=limit(24),
    )(core, pltpu.with_memory_space_constraint(snapshots.reshape(pieces * rows, window), pltpu.HBM))


def split_halves(core_ref, total, mine_ref, other_ref):
    first = core_ref[0] == 0
    rows = total.shape[0] // 2
    mine_ref[...] = jnp.where(first, total[:rows], total[rows:])
    other_ref[...] = jnp.where(first, total[rows:], total[:rows])


def join_halves(core_ref, mine_ref, other_ref, scale):
    first = core_ref[0] == 0
    mine, other = mine_ref[...] * scale, other_ref[...] * scale
    return jnp.concatenate([jnp.where(first, mine, other), jnp.where(first, other, mine)])


def time_subspace(core, mine, other, start, scale):
    rank, window = start.shape

    def kernel(core_ref, mine_ref, other_ref, start_ref, basis_ref, pair_ref, held_ref):
        held_ref[...] = join_halves(core_ref, mine_ref, other_ref, scale)
        joined_sweeps(held_ref, start_ref[...], ITT, basis_ref)
        narrow = basis_ref[...].T.astype(BF16)
        zero = jnp.zeros_like(narrow)
        pair_ref[:window] = jnp.concatenate([narrow, zero], axis=1)
        pair_ref[window:] = jnp.concatenate([zero, narrow], axis=1)

    return pl.pallas_call(
        kernel,
        in_specs=[SMEM, VMEM, VMEM, VMEM],
        out_specs=[VMEM, VMEM],
        out_shape=[
            jax.ShapeDtypeStruct((rank, window), F32),
            jax.ShapeDtypeStruct((2 * window, 2 * rank), BF16),
        ],
        scratch_shapes=[pltpu.VMEM((window, window), F32)],
        compiler_params=limit(6),
    )(core, mine, other, start)


def truncate_time(shape, near, pair_basis, owners):
    variables, planes, cells, window = shape
    half = variables // 2
    lanes = pair_basis.shape[1]
    own = cells // owners

    def kernel(near_ref, basis_ref, out_ref):
        basis = basis_ref[...]
        for v in range(half):
            for x in range(planes):
                low, high = [((v + side) * planes + x) * cells for side in (0, half)]
                both = jnp.concatenate(
                    [near_ref[low : low + cells], near_ref[high : high + cells]], axis=1
                )
                core = narrow_product(both, basis, 1, 0).astype(BF16)
                out_ref[:, x, v] = core.reshape(owners, own, lanes)

    return pl.pallas_call(
        kernel,
        in_specs=[VMEM, VMEM],
        out_specs=VMEM,
        out_shape=jax.ShapeDtypeStruct((owners, planes, half, own, lanes), BF16),
        compiler_params=limit(24),
    )(pltpu.with_memory_space_constraint(near, pltpu.VMEM), pair_basis)


def plane_gram(core, pencils):
    planes, groups, lanes = pencils.shape

    def kernel(core_ref, pencil_ref, mine_ref, other_ref, group_ref, held, sent):
        total, sends = None, []
        for i in range(0, groups, 16):
            turned = jnp.swapaxes(pencil_ref[:, i : i + 16], 0, 1)
            place = pl.ds(i, 16)
            held[place] = turned
            sends.append(pltpu.make_async_copy(held.at[place], group_ref.at[place], sent.at[i // 16]))
            sends[-1].start()
            for j in range(0, 16, 2):
                both = jnp.concatenate([turned[j], turned[j + 1]], axis=1)
                part = narrow_product(both, both, 1, 1)
                total = part if total is None else total + part
        split_halves(core_ref, total, mine_ref, other_ref)
        for send in sends:
            send.wait()

    half = jax.ShapeDtypeStruct((planes // 2, planes), F32)
    return pl.pallas_call(
        kernel,
        in_specs=[SMEM, VMEM],
        out_specs=[VMEM, VMEM, HBM],
        out_shape=[half, half, pltpu.HBM((groups, planes, lanes), BF16)],
        scratch_shapes=[
            pltpu.VMEM((groups, planes, lanes), BF16),
            pltpu.SemaphoreType.DMA((groups // 16,)),
        ],
        compiler_params=limit(24),
    )(core, pencils)


def plane_subspace(core, mine, other, start, groups, scale, half):
    rank, planes = start.shape
    count, _, lanes = groups.shape
    own = count // half
    ranks = lanes // 2

    def kernel(core_ref, mine_ref, other_ref, start_ref, far_ref, basis_ref, out_ref, group_ref, arrived, held_ref):
        fetch = pltpu.make_async_copy(far_ref, group_ref, arrived)
        fetch.start()
        held_ref[...] = join_halves(core_ref, mine_ref, other_ref, scale)
        joined_sweeps(held_ref, start_ref[...], ITX, basis_ref)
        narrow = basis_ref[...].astype(BF16)
        fetch.wait()
        first = lax.broadcasted_iota(jnp.int32, (rank, lanes), 1) < ranks
        for v in range(half):
            for pair in range(own // 2):
                even = narrow_product(narrow, group_ref[v * own + 2 * pair], 1, 0)
                odd = narrow_product(narrow, group_ref[v * own + 2 * pair + 1], 1, 0)
                low = jnp.where(first, even, pltpu.roll(odd, ranks, 1))
                high = jnp.where(first, pltpu.roll(even, ranks, 1), odd)
                place = slice(pair * lanes, (pair + 1) * lanes)
                out_ref[v, :, place] = low.astype(BF16)
                out_ref[v + half, :, place] = high.astype(BF16)

    return pl.pallas_call(
        kernel,
        in_specs=[SMEM, VMEM, VMEM, VMEM, HBM],
        out_specs=[VMEM, VMEM],
        out_shape=[
            jax.ShapeDtypeStruct((rank, planes), F32),
            jax.ShapeDtypeStruct((2 * half, rank, own * ranks), BF16),
        ],
        scratch_shapes=[
            pltpu.VMEM(groups.shape, BF16),
            pltpu.SemaphoreType.DMA,
            pltpu.VMEM((planes, planes), F32),
        ],
        compiler_params=limit(16),
    )(core, mine, other, start, pltpu.with_memory_space_constraint(groups, pltpu.HBM))


def on_device(snapshots, start_time, start_plane):
    variables, planes, cells, window = snapshots.shape
    devices_all = lax.axis_size("blk") * lax.axis_size("pen")
    half = variables // 2
    rank = start_time.shape[1]
    torus = Torus()
    core = torus.core.reshape(1)

    mine, other, near = time_gram(core, snapshots)
    total = mine + torus.swap_cores(other)
    for stage in range(3):
        total = torus.all_sum(total, stage)
    scale_time = 1.0 / float(variables * planes * cells * devices_all)
    time_basis, pair_basis = time_subspace(
        core, total, torus.swap_cores(total), start_time.T, scale_time
    )

    core_time = truncate_time(snapshots.shape, near, pair_basis, devices_all)
    pencils = lax.all_to_all(core_time, ("blk", "pen"), split_axis=0, concat_axis=0, tiled=True)
    mine, other, groups = plane_gram(core, pencils.reshape(devices_all * planes, -1, 2 * rank))

    total = mine + torus.swap_cores(other)
    total = torus.scatter_sum(total, 0)
    for stage in (1, 2):
        total = torus.all_sum(total, stage)
    total = torus.gather(total, 0)
    scale_plane = 1.0 / float(variables * cells * rank)
    plane_basis, core_tensor = plane_subspace(
        core, total, torus.swap_cores(total), start_plane.T, groups, scale_plane, half
    )
    return (time_basis.T, plane_basis.T, core_tensor)


def solution(mesh):
    return jax.shard_map(
        on_device,
        mesh=mesh,
        in_specs=(P(None, ("blk", "pen"), None, None), P(), P()),
        out_specs=(P(), P(), P(None, None, ("blk", "pen"))),
        check_vma=False,
    )
```

```python
import jax
import jax.numpy as jnp
from jax import lax
from jax.experimental import pallas as pl
from jax.experimental.pallas import tpu as pltpu
from jax.sharding import PartitionSpec as P

ITT = 3
ITX = 3

F32, BF16 = jnp.float32, jnp.bfloat16
PIVOT_FLOOR = 1e-5
HIGHEST = lax.Precision.HIGHEST
VMEM = pl.BlockSpec(memory_space=pltpu.VMEM)
SMEM = pl.BlockSpec(memory_space=pltpu.SMEM)
HBM = pl.BlockSpec(memory_space=pltpu.HBM)


class Torus:
    orders = ("xyz", "zxy")
    steps = (2, 3, 1)

    def __init__(self):
        self.blk = lax.axis_size("blk")
        self.pen = lax.axis_size("pen")
        index = lax.axis_index("blk")
        self.core = index % 2
        self.place = {"x": lax.axis_index("pen"), "y": (index // 2) % 4, "z": index // 8}

    def partners(self, stage, step):
        pairs = []
        for blk in range(self.blk):
            axis = "core" if stage is None else self.orders[blk % 2][stage]
            for pen in range(self.pen):
                to_pen = pen ^ step if axis == "x" else pen
                to_blk = blk ^ (step * {"core": 1, "x": 0, "y": 2, "z": 8}[axis])
                pairs.append((blk * self.pen + pen, to_blk * self.pen + to_pen))
        return pairs

    def swap(self, value, stage, step):
        return lax.ppermute(value, ("blk", "pen"), self.partners(stage, step))

    def swap_cores(self, value):
        return self.swap(value, None, 1)

    def stage_place(self, stage):
        first, second = [self.place[order[stage]] for order in self.orders]
        return jnp.where(self.core == 0, first, second)

    def all_sum(self, value, stage):
        got = {step: self.swap(value, stage, step) for step in self.steps}
        return (value + got[1]) + (got[2] + got[3])

    def scatter_sum(self, value, stage):
        pieces = value.reshape((4, value.shape[0] // 4) + value.shape[1:])
        place = self.stage_place(stage)
        take = lambda step: lax.dynamic_index_in_dim(pieces, place ^ step, 0, False)
        got = {step: self.swap(take(step), stage, step) for step in self.steps}
        return (take(0) + got[1]) + (got[2] + got[3])

    def gather(self, value, stage):
        place = self.stage_place(stage)
        result = jnp.zeros((4,) + value.shape, value.dtype)
        for step in (0,) + self.steps:
            piece = value if step == 0 else self.swap(value, stage, step)
            result = lax.dynamic_update_index_in_dim(result, piece, place ^ step, 0)
        return result.reshape((4 * value.shape[0],) + value.shape[1:])


def limit(mebibytes):
    return pltpu.CompilerParams(vmem_limit_bytes=mebibytes << 20)


def product(a, b, dim_a, dim_b, precision=HIGHEST):
    dims = (((dim_a,), (dim_b,)), ((), ()))
    return lax.dot_general(a, b, dims, precision=precision, preferred_element_type=F32)


def narrow_product(a, b, dim_a, dim_b):
    return product(a, b, dim_a, dim_b, None)


def identity(size):
    shape = (size, size)
    same = lax.broadcasted_iota(jnp.int32, shape, 0) == lax.broadcasted_iota(jnp.int32, shape, 1)
    return jnp.where(same, 1.0, 0.0).astype(F32)


def inverse_factor(square):
    size = square.shape[0]
    blocks = size // 8
    wide = jnp.concatenate([square, identity(size)], axis=1)
    rows = [wide[8 * i : 8 * i + 8] for i in range(blocks)]
    place = lax.broadcasted_iota(jnp.int32, (8, 1), 0)
    for block in range(blocks):
        columns = slice(8 * block, 8 * block + 8)
        splats = {
            i: [jnp.broadcast_to(rows[i][:, columns][:, j : j + 1], wide[:8].shape) for j in range(8)]
            for i in range(block, blocks)
        }
        pivots = splats[block]
        done = []
        for j in range(8):
            root = lax.rsqrt(pivots[j][j : j + 1])
            scaled = rows[block][j : j + 1] * root
            factors = {i: splats[i][j] * root for i in splats}
            factors[block] = jnp.where(place > j, factors[block], 0.0)
            pivot_row = {m: pivots[m][j : j + 1] * root for m in range(j + 1, 8)}
            for i in splats:
                rows[i] = rows[i] - factors[i] * scaled
                for m in pivot_row:
                    splats[i][m] = splats[i][m] - factors[i] * pivot_row[m]
            done.append(scaled)
        rows[block] = jnp.concatenate(done, axis=0)
    return jnp.concatenate(rows, axis=0)[:, size:]


def orthonormal_round(flat):
    square = product(flat, flat, 1, 1)
    inverse = inverse_factor(square)
    same = identity(square.shape[0])
    lead = jnp.sum(inverse * same, axis=1, keepdims=True)
    diagonal = jnp.sum(square * same, axis=1, keepdims=True)
    weak = jnp.where(lead * lead * diagonal * PIVOT_FLOOR < 1.0, 0.0, 1.0)
    return product(inverse, flat, 1, 0), jnp.sum(weak)


def joined_sweeps(gram_ref, start, sweeps, flat_ref):
    gram = gram_ref[...]
    flat = start
    for sweep in range(sweeps - 2):
        flat = orthonormal_round(product(flat, gram, 1, 0))[0]
    flat = product(product(flat, gram, 1, 0), gram, 1, 0)
    flat, weak = orthonormal_round(flat)
    flat_ref[...] = orthonormal_round(flat)[0]

    @pl.when(weak > 0.0)
    def _():
        flat_ref[...] = start

        @pl.loop(0, sweeps + 1)
        def _(index):
            @pl.when(index < sweeps)
            def _():
                flat_ref[...] = product(flat_ref[...], gram_ref[...], 1, 0)

            flat_ref[...] = orthonormal_round(flat_ref[...])[0]


def time_gram(core, snapshots):
    variables, planes, cells, window = snapshots.shape
    pieces = 8
    rows = variables * planes * cells // pieces

    def kernel(core_ref, far_ref, mine_ref, other_ref, near_ref, arrived):
        fetches = []
        for i in range(pieces):
            place = pl.ds(i * rows, rows)
            fetches.append(
                pltpu.make_async_copy(far_ref.at[place], near_ref.at[place], arrived.at[i])
            )
            fetches[-1].start()
        total = None
        for i in range(pieces):
            fetches[i].wait()
            first, second = [
                near_ref[i * rows + j * rows // 2 : i * rows + (j + 1) * rows // 2] for j in range(2)
            ]
            both = jnp.concatenate([first, second], axis=1)
            part = narrow_product(both, both, 0, 0)
            total = part if total is None else total + part
        total = total[:window, :window] + total[window:, window:]
        split_halves(core_ref, total, mine_ref, other_ref)

    half = jax.ShapeDtypeStruct((window // 2, window), F32)
    return pl.pallas_call(
        kernel,
        in_specs=[SMEM, HBM],
        out_specs=[VMEM, VMEM, VMEM],
        out_shape=[half, half, pltpu.VMEM((pieces * rows, window), BF16)],
        scratch_shapes=[pltpu.SemaphoreType.DMA((pieces,))],
        compiler_params=limit(24),
    )(core, pltpu.with_memory_space_constraint(snapshots.reshape(pieces * rows, window), pltpu.HBM))


def split_halves(core_ref, total, mine_ref, other_ref):
    first = core_ref[0] == 0
    rows = total.shape[0] // 2
    mine_ref[...] = jnp.where(first, total[:rows], total[rows:])
    other_ref[...] = jnp.where(first, total[rows:], total[:rows])


def join_halves(core_ref, mine_ref, other_ref, scale):
    first = core_ref[0] == 0
    mine, other = mine_ref[...] * scale, other_ref[...] * scale
    return jnp.concatenate([jnp.where(first, mine, other), jnp.where(first, other, mine)])


def time_subspace(core, mine, other, start, scale):
    rank, window = start.shape

    def kernel(core_ref, mine_ref, other_ref, start_ref, basis_ref, pair_ref, held_ref):
        held_ref[...] = join_halves(core_ref, mine_ref, other_ref, scale)
        joined_sweeps(held_ref, start_ref[...], ITT, basis_ref)
        narrow = basis_ref[...].T.astype(BF16)
        zero = jnp.zeros_like(narrow)
        pair_ref[:window] = jnp.concatenate([narrow, zero], axis=1)
        pair_ref[window:] = jnp.concatenate([zero, narrow], axis=1)

    return pl.pallas_call(
        kernel,
        in_specs=[SMEM, VMEM, VMEM, VMEM],
        out_specs=[VMEM, VMEM],
        out_shape=[
            jax.ShapeDtypeStruct((rank, window), F32),
            jax.ShapeDtypeStruct((2 * window, 2 * rank), BF16),
        ],
        scratch_shapes=[pltpu.VMEM((window, window), F32)],
        compiler_params=limit(6),
    )(core, mine, other, start)


def truncate_time(shape, near, pair_basis, owners):
    variables, planes, cells, window = shape
    half = variables // 2
    lanes = pair_basis.shape[1]
    own = cells // owners

    def kernel(near_ref, basis_ref, out_ref):
        basis = basis_ref[...]
        for v in range(half):
            for x in range(planes):
                low, high = [((v + side) * planes + x) * cells for side in (0, half)]
                both = jnp.concatenate(
                    [near_ref[low : low + cells], near_ref[high : high + cells]], axis=1
                )
                core = narrow_product(both, basis, 1, 0).astype(BF16)
                out_ref[:, x, v] = core.reshape(owners, own, lanes)

    return pl.pallas_call(
        kernel,
        in_specs=[VMEM, VMEM],
        out_specs=VMEM,
        out_shape=jax.ShapeDtypeStruct((owners, planes, half, own, lanes), BF16),
        compiler_params=limit(24),
    )(pltpu.with_memory_space_constraint(near, pltpu.VMEM), pair_basis)


def plane_gram(core, pencils):
    planes, groups, lanes = pencils.shape

    def kernel(core_ref, pencil_ref, mine_ref, other_ref, group_ref, held, sent):
        total, sends = None, []
        for i in range(0, groups, 16):
            turned = jnp.swapaxes(pencil_ref[:, i : i + 16], 0, 1)
            place = pl.ds(i, 16)
            held[place] = turned
            sends.append(pltpu.make_async_copy(held.at[place], group_ref.at[place], sent.at[i // 16]))
            sends[-1].start()
            for j in range(0, 16, 2):
                both = jnp.concatenate([turned[j], turned[j + 1]], axis=1)
                part = narrow_product(both, both, 1, 1)
                total = part if total is None else total + part
        split_halves(core_ref, total, mine_ref, other_ref)
        for send in sends:
            send.wait()

    half = jax.ShapeDtypeStruct((planes // 2, planes), F32)
    return pl.pallas_call(
        kernel,
        in_specs=[SMEM, VMEM],
        out_specs=[VMEM, VMEM, HBM],
        out_shape=[half, half, pltpu.HBM((groups, planes, lanes), BF16)],
        scratch_shapes=[
            pltpu.VMEM((groups, planes, lanes), BF16),
            pltpu.SemaphoreType.DMA((groups // 16,)),
        ],
        compiler_params=limit(24),
    )(core, pencils)


def plane_subspace(core, mine, other, start, groups, scale, half):
    rank, planes = start.shape
    count, _, lanes = groups.shape
    own = count // half
    ranks = lanes // 2

    def kernel(core_ref, mine_ref, other_ref, start_ref, far_ref, basis_ref, out_ref, group_ref, arrived, held_ref):
        fetch = pltpu.make_async_copy(far_ref, group_ref, arrived)
        fetch.start()
        held_ref[...] = join_halves(core_ref, mine_ref, other_ref, scale)
        joined_sweeps(held_ref, start_ref[...], ITX, basis_ref)
        narrow = basis_ref[...].astype(BF16)
        fetch.wait()
        first = lax.broadcasted_iota(jnp.int32, (rank, lanes), 1) < ranks
        for v in range(half):
            for pair in range(own // 2):
                even = narrow_product(narrow, group_ref[v * own + 2 * pair], 1, 0)
                odd = narrow_product(narrow, group_ref[v * own + 2 * pair + 1], 1, 0)
                low = jnp.where(first, even, pltpu.roll(odd, ranks, 1))
                high = jnp.where(first, pltpu.roll(even, ranks, 1), odd)
                place = slice(pair * lanes, (pair + 1) * lanes)
                out_ref[v, :, place] = low.astype(BF16)
                out_ref[v + half, :, place] = high.astype(BF16)

    return pl.pallas_call(
        kernel,
        in_specs=[SMEM, VMEM, VMEM, VMEM, HBM],
        out_specs=[VMEM, VMEM],
        out_shape=[
            jax.ShapeDtypeStruct((rank, planes), F32),
            jax.ShapeDtypeStruct((2 * half, rank, own * ranks), BF16),
        ],
        scratch_shapes=[
            pltpu.VMEM(groups.shape, BF16),
            pltpu.SemaphoreType.DMA,
            pltpu.VMEM((planes, planes), F32),
        ],
        compiler_params=limit(16),
    )(core, mine, other, start, pltpu.with_memory_space_constraint(groups, pltpu.HBM))


def on_device(snapshots, start_time, start_plane):
    variables, planes, cells, window = snapshots.shape
    devices_all = lax.axis_size("blk") * lax.axis_size("pen")
    half = variables // 2
    rank = start_time.shape[1]
    torus = Torus()
    core = torus.core.reshape(1)

    mine, other, near = time_gram(core, snapshots)
    total = mine + torus.swap_cores(other)
    for stage in range(3):
        total = torus.all_sum(total, stage)
    scale_time = 1.0 / float(variables * planes * cells * devices_all)
    time_basis, pair_basis = time_subspace(
        core, total, torus.swap_cores(total), start_time.T, scale_time
    )

    core_time = truncate_time(snapshots.shape, near, pair_basis, devices_all)
    pencils = lax.all_to_all(core_time, ("blk", "pen"), split_axis=0, concat_axis=0, tiled=True)
    mine, other, groups = plane_gram(core, pencils.reshape(devices_all * planes, -1, 2 * rank))

    total = mine + torus.swap_cores(other)
    total = torus.scatter_sum(total, 0)
    for stage in (1, 2):
        total = torus.all_sum(total, stage)
    total = torus.gather(total, 0)
    scale_plane = 1.0 / float(variables * cells * rank)
    plane_basis, core_tensor = plane_subspace(
        core, total, torus.swap_cores(total), start_plane.T, groups, scale_plane, half
    )
    return (time_basis.T, plane_basis.T, core_tensor)


def solution(mesh):
    return jax.shard_map(
        on_device,
        mesh=mesh,
        in_specs=(P(None, ("blk", "pen"), None, None), P(), P()),
        out_specs=(P(), P(), P(None, None, ("blk", "pen"))),
        check_vma=False,
    )
```
